32 devices in a mesh: section: 4 (over y, core), expert: 8 (over z, x).
Axes of the slice: x: 2, y: 2, z: 4, core: 2. Of those that a mesh axis runs over, the one named last changes fastest.
Arguments:
- acts: bfloat16 [4, 512, 2048], P('section', 'expert'), may hold values from -6 to 6
- norm_gains: float32 [4, 2, 2048], P('section'), may hold values from 0.5 to 5.5
- w_query: bfloat16 [4, 2048, 1024], P('section', None, 'expert'), may hold values from -0.125 to 0.125
- w_keyval: bfloat16 [4, 2048, 4, 256], P('section', 'expert'), may hold values from -0.125 to 0.125
- w_out: bfloat16 [4, 1024, 2048], P('section', 'expert'), may hold values from -0.5 to 0.5
- w_gate_up: bfloat16 [4, 32, 2048, 1536], P('section', 'expert'), may hold values from -0.125 to 0.125
- w_down: bfloat16 [4, 32, 768, 2048], P('section', 'expert'), may hold values from -0.21875 to 0.21875
- expert_ids: int32 [4, 512, 8], P('section', 'expert'), may hold values from 0 to 31, all different within a row; in each aligned block of 64 rows (0 to 63, 64 to 127, ..., all dimensions but the last counted through in order) at most 24 rows name the same one
- gate_weights: float32 [4, 512, 8], P('section', 'expert'), may hold values from 0.05 to 0.3
- segment_ids: int32 [4, 512], P('section'), may hold values from 0 to 15, never falling along the last dimension, each value on 1 to 128 neighbouring positions
Outputs:
- handed: bfloat16 [4, 512, 2048], P('section', 'expert')
The draws below stay inside these ranges and needn't reach their ends.
Inputs may be any that keep to these rules, and one draw needn't show every extreme that they name: `expert_ids`: A token names 8 different experts. In each section the tokens of one index of expert (aligned blocks of 64 tokens) name no expert more than 24 times, a bound that some block reaches. `segment_ids`: never falling along a section's positions; a segment holds at most 128 positions, and one exactly that many.
All inputs are finite; a program needn't handle non-finite values.
Results may differ from the reference program's by a relative error of at most 0.015.
The reference program's roundings to bfloat16 on the way count: a program that leaves them out, or rounds other values in their place, can miss the bound.
Values may be sent and summed in bfloat16 or wider, within the bound.
A program may use at most 128 MiB of HBM per device.

```python
import math
import jax
import jax.numpy as jnp
import numpy as np
from jax import lax

D = 2048
HD = 128
HEAD_DEV = 1
KV = 4
FF = 768
EXPERTS = 32
TOPK = 8
TOK_DEV = 64
HEADS = 8
CAP = 24
TOKENS = 512
SECTIONS = 4
N_EXPERT = 8


def draw_norm_gains(key, part):
    first_key, second_key = jax.random.split(key)
    attention_gain = jax.random.uniform(first_key, (SECTIONS, 1, D), jnp.float32, 0.6, 1.4)
    mixer_gain = jax.random.uniform(second_key, (SECTIONS, 1, D), jnp.float32, 0.6, 1.4)
    return jnp.concatenate([attention_gain, mixer_gain], axis=1)


def shard_levels(stream_key, dims, shards, low, high):
    factor_of, own = 1.0, jax.random.fold_in(stream_key, 6)
    for axis_at, blocks in shards:
        steps = jnp.exp(jax.random.uniform(jax.random.fold_in(own, axis_at), (blocks,), jnp.float32, low / len(shards), high / len(shards)))
        factor_of = factor_of * jnp.repeat(steps, dims[axis_at] // blocks).reshape([-1 if axis == axis_at else 1 for axis in range(len(dims))])
    return factor_of


def length_profile(count, total, limit, slope):
    loads = [(1 << 20) // math.isqrt(rank ** slope) + 1 for rank in range(2, count + 1)]
    rest, holding = total - limit - (count - 1), [1] * (count - 1)
    while rest > 0:
        movable = [i for i in range(count - 1) if holding[i] < limit]
        whole, left = sum([loads[i] for i in movable]), rest
        for i in movable:
            more = min(limit - holding[i], max(1, left * loads[i] // whole), rest)
            holding[i] = holding[i] + more
            rest = rest - more
    return np.array([limit] + holding)


def ragged_sizes(own_key, count, total, bound, slope):
    if count == 2:
        one = jax.random.randint(own_key, (), max(1, total - bound), min(bound, total - 1) + 1)
        return jnp.stack([one, total - one])
    lengths = jnp.asarray(length_profile(count, total, bound, slope), jnp.int32)
    twos = (count - 1) // 2
    donor, taker = lengths[1:1 + 2 * twos:2], lengths[2:2 + 2 * twos:2]
    room = jnp.minimum(donor - 1, bound - taker)
    moved = jax.random.randint(jax.random.fold_in(own_key, 1), (twos,), 0, 1 << 20) % (room + 1)
    lengths = lengths.at[1:1 + 2 * twos:2].set(donor - moved).at[2:2 + 2 * twos:2].set(taker + moved)
    return lengths[jax.random.permutation(jax.random.fold_in(own_key, 2), count)]


def shared_out(key, own, number, rows, number_of, top, bound, skew):
    order = jax.random.permutation(key, number_of)
    crowded, usual = portions_of(number_of, rows * top, bound, skew, True), portions_of(number_of, rows * top, bound, skew, False)
    places = jnp.arange(number_of)

    def named(lengths, offset_by):
        used = int((lengths > 0).sum())
        fixed = max(1, used // 4)
        passed = fixed + (places - fixed + offset_by * (used - fixed)) % max(1, number_of - fixed)
        return jnp.zeros((number_of,), jnp.int32).at[order[jnp.where(places < fixed, places, passed)]].set(jnp.asarray(lengths, jnp.int32))

    lengths = jnp.where(number % 4 == 0, named(crowded, number // 4), named(usual, number - number // 4 - 1))
    mixed = jax.random.permutation(jax.random.fold_in(own, 3), number_of)
    source_of, taker = mixed[0:number_of // 2 * 2:2], mixed[1:number_of // 2 * 2:2]
    slack = jnp.minimum(lengths[source_of] - 1, bound - lengths[taker]) // 2
    slack = jnp.where((source_of == order[0]) | (taker == order[0]) | (lengths[taker] == 0), 0, jnp.maximum(slack, 0))
    passed = jax.random.randint(jax.random.fold_in(own, 4), (number_of // 2,), 0, 1 << 20) % (slack + 1)
    lengths = lengths.at[source_of].add(-passed).at[taker].add(passed)
    members = jnp.searchsorted(jnp.cumsum(lengths), jnp.arange(rows * top), side="right").astype(jnp.int32)
    grid = members.reshape(top, rows).T
    grid = grid[jax.random.permutation(jax.random.fold_in(own, 1), rows)]
    offset_by = jax.random.randint(jax.random.fold_in(own, 2), (rows, 1), 0, top)
    return jnp.take_along_axis(grid, (jnp.arange(top)[None, :] + offset_by) % top, axis=1)


def portions_of(number_of, total, limit, slope, full):
    weights = [(1 << 20) // math.isqrt(standing ** slope) + 1 for standing in range(1, number_of + 1)]
    largest = limit if full else min(limit, max(-(-total // number_of), total * weights[0] // sum(weights)))
    least = 1 if total - largest >= number_of - 1 else 0
    given, spare = [largest] + [least] * (number_of - 1), total - largest - least * (number_of - 1)
    while spare > 0:
        free = [i for i in range(1, number_of) if given[i] < largest] or [i for i in range(1, number_of) if given[i] < limit]
        whole, remaining = sum([weights[i] for i in free]), spare
        for i in free:
            extra = min(limit - given[i], max(1, remaining * weights[i] // whole), spare)
            given[i] = given[i] + extra
            spare = spare - extra
    return np.array(given)


def normal_values(stream_key, dims, width, reach, cuts=(), kind=jnp.bfloat16):
    array = width * jax.random.normal(stream_key, dims, jnp.float32)
    if cuts:
        array = array * shard_levels(stream_key, dims, cuts, -0.22, 0.18)
    return jnp.clip(array, -reach, reach).astype(kind)


def setup_inputs(seed: int = 0) -> dict:
    key_list = jax.random.split(jax.random.key(seed), 11)
    acts = normal_values(key_list[0], (SECTIONS, TOKENS, D), 1.0, 6.0, ((0, 4), (1, 8)))
    norm_gains = draw_norm_gains(jax.random.fold_in(key_list[10], 71), 0)
    w_query = normal_values(key_list[2], (SECTIONS, D, HEADS * HD), D ** -0.5, 0.125, ((0, 4), (2, 8)))
    w_keyval = normal_values(key_list[3], (SECTIONS, D, KV, 2 * HD), D ** -0.5, 0.125, ((0, 4), (1, 8)))
    w_out = normal_values(key_list[4], (SECTIONS, HEADS * HD, D), HD ** -0.5, 0.5, ((0, 4), (1, 8)))
    w_gate_up = normal_values(key_list[5], (SECTIONS, EXPERTS, D, 2 * FF), D ** -0.5, 0.125, ((0, 4), (1, 8)))
    w_down = normal_values(key_list[6], (SECTIONS, EXPERTS, FF, D), FF ** -0.5, 0.21875, ((0, 4), (1, 8)))
    expert_ids_keys = jax.random.split(jax.random.fold_in(key_list[7], 1), SECTIONS * TOKENS // TOK_DEV)
    expert_ids_turns = jax.random.permutation(jax.random.fold_in(key_list[7], 3), SECTIONS * TOKENS // TOK_DEV)
    expert_ids = jax.vmap(lambda own, number: shared_out(jax.random.fold_in(key_list[7], 2), own, number, TOK_DEV, EXPERTS, TOPK, CAP, 2))(expert_ids_keys, expert_ids_turns).reshape((SECTIONS, TOKENS, TOPK))
    gate_weights = jnp.clip(0.05 + 0.25 * jax.random.uniform(key_list[8], (SECTIONS, TOKENS, TOPK), jnp.float32) ** shard_levels(key_list[8], (SECTIONS, TOKENS, TOPK), ((0, 4), (1, 8)), -0.2, 0.2), 0.05, 0.3)
    segment_ids = jax.vmap(lambda own: jnp.searchsorted(jnp.cumsum(ragged_sizes(own, 16, TOKENS, TOKENS // 4, 2)), jnp.arange(TOKENS), side="right"))(jax.random.split(key_list[9], SECTIONS)).reshape((SECTIONS, TOKENS)).astype(jnp.int32)
    return dict(acts=acts, norm_gains=norm_gains, w_query=w_query, w_keyval=w_keyval, w_out=w_out, w_gate_up=w_gate_up, w_down=w_down, expert_ids=expert_ids, gate_weights=gate_weights, segment_ids=segment_ids)


EPS = 1e-06
ROPE_BASE = 1000000.0

def rms_scale(values, gain_row):
    mean_sq = lax.optimization_barrier(jnp.mean(values * values, axis=-1, keepdims=True))
    return values * lax.rsqrt(mean_sq + EPS) * gain_row

def rotate(values, positions):
    half_width = values.shape[-1] // 2
    frequency = ROPE_BASE ** (-jnp.arange(half_width, dtype=jnp.float32) * 2.0 / values.shape[-1])
    angles = positions[:, None] * frequency[None, :]
    cosines = jnp.cos(angles)[:, None, :]
    sine_table = jnp.sin(angles)[:, None, :]
    leading = values[..., :half_width]
    trailing = values[..., half_width:]
    return jnp.concatenate([leading * cosines - trailing * sine_table, trailing * cosines + leading * sine_table], axis=-1)

def section_layer(inputs, gains, w_query, w_keyval, w_out, w_gate_up, w_down, expert_ids, gate_weights, segment_ids):
    tokens = inputs.shape[0]
    x_wide = inputs.astype(jnp.float32)
    normed = rms_scale(x_wide, gains[0]).astype(jnp.bfloat16)
    positions = jnp.arange(tokens).astype(jnp.float32)
    queries = jnp.dot(normed, w_query, preferred_element_type=jnp.float32).reshape(tokens, HEADS, HD)
    queries = rotate(queries, positions).astype(jnp.bfloat16)
    keyval = jnp.dot(normed, w_keyval.reshape(D, KV * 2 * HD), preferred_element_type=jnp.float32).reshape(tokens, KV, 2 * HD)
    key_rows = rotate(keyval[:, :, :HD], positions).astype(jnp.bfloat16)
    value_rows = keyval[:, :, HD:].astype(jnp.bfloat16)
    token_order = jnp.arange(tokens)
    allowed = (segment_ids[:, None] == segment_ids[None, :]) & (token_order[None, :] <= token_order[:, None])
    group_size = HEADS // KV
    score_scale = 1.0 / math.sqrt(HD)
    queries_by_head = queries.transpose(1, 0, 2)
    keys_by_head = key_rows.transpose(1, 0, 2)
    values_by_head = value_rows.transpose(1, 0, 2)

    def one_head(head_pack):
        q_head, head_index = head_pack
        kv_index = head_index // group_size
        k_head = lax.dynamic_index_in_dim(keys_by_head, kv_index, 0, keepdims=False)
        v_head = lax.dynamic_index_in_dim(values_by_head, kv_index, 0, keepdims=False)
        scores = jnp.dot(q_head, k_head.T, preferred_element_type=jnp.float32) * score_scale
        scores = jnp.where(allowed, scores, -1e+30)
        row_max = lax.optimization_barrier(jnp.max(scores, axis=-1, keepdims=True))
        shifted = jnp.exp(scores - row_max)
        probability = (shifted / lax.optimization_barrier(jnp.sum(shifted, axis=-1, keepdims=True))).astype(jnp.bfloat16)
        return jnp.dot(probability, v_head, preferred_element_type=jnp.float32).astype(jnp.bfloat16)
    heads_out = lax.map(one_head, (queries_by_head, jnp.arange(HEADS).astype(jnp.int32)))

    def add_share(total, share_pair):
        head_part, weights = share_pair
        flat_heads = head_part.transpose(1, 0, 2).reshape(tokens, HEAD_DEV * HD)
        partial_value = jnp.dot(flat_heads, weights, preferred_element_type=jnp.float32).astype(jnp.bfloat16)
        partial_value = lax.optimization_barrier(partial_value)
        return (total + partial_value.astype(jnp.float32), None)
    attention, _ = lax.scan(add_share, jnp.zeros((tokens, D), jnp.float32), (heads_out.reshape(N_EXPERT, HEAD_DEV, tokens, HD), w_out.reshape(N_EXPERT, HEAD_DEV * HD, D)))
    middle = (x_wide + attention).astype(jnp.bfloat16)
    middle_wide = middle.astype(jnp.float32)
    mixer_in = rms_scale(middle_wide, gains[1]).astype(jnp.bfloat16)
    rows_dev = TOK_DEV * TOPK
    routes_flat = expert_ids.reshape(N_EXPERT, rows_dev)
    onehot = (routes_flat[:, :, None] == jnp.arange(EXPERTS, dtype=jnp.int32)[None, None, :]).astype(jnp.int32)
    earlier = jnp.cumsum(onehot, axis=1) - onehot
    slot_rank = lax.optimization_barrier(jnp.sum(earlier * onehot, axis=2))
    source = jnp.arange(N_EXPERT, dtype=jnp.int32)[:, None]
    slot_index = ((routes_flat * N_EXPERT + source) * CAP + slot_rank).reshape(-1)
    routed = jnp.repeat(mixer_in, TOPK, axis=0)
    buffer = jnp.zeros((EXPERTS * N_EXPERT * CAP, D), jnp.bfloat16).at[slot_index].set(routed)
    buffer = buffer.reshape(EXPERTS, N_EXPERT * CAP, D)

    def run_expert(expert_pack):
        slot_rows, gate_up, down_proj = expert_pack
        gate_up_out = jnp.dot(slot_rows, gate_up, preferred_element_type=jnp.float32)
        hidden = (jax.nn.silu(gate_up_out[:, :FF]) * gate_up_out[:, FF:]).astype(jnp.bfloat16)
        return jnp.dot(hidden, down_proj, preferred_element_type=jnp.float32).astype(jnp.bfloat16)
    outputs = lax.map(run_expert, (buffer, w_gate_up, w_down))
    picked = outputs.reshape(-1, D)[slot_index].astype(jnp.float32).reshape(tokens, TOPK, D)
    mixed = lax.optimization_barrier(jnp.sum(picked * gate_weights[:, :, None], axis=1))
    return (middle_wide + mixed).astype(jnp.bfloat16)

def reference(acts, norm_gains, w_query, w_keyval, w_out, w_gate_up, w_down, expert_ids, gate_weights, segment_ids):
    results = []
    for section_index in range(acts.shape[0]):
        results.append(section_layer(acts[section_index], norm_gains[section_index], w_query[section_index], w_keyval[section_index], w_out[section_index], w_gate_up[section_index], w_down[section_index], expert_ids[section_index], gate_weights[section_index], segment_ids[section_index]))
    return jnp.roll(jnp.stack(results), 1, axis=0)
```

```python
import math

import jax
import jax.numpy as jnp
from jax import lax
from jax.experimental import pallas as pl
from jax.experimental.pallas import tpu as pltpu
from jax.sharding import PartitionSpec as P

MESH = pl.DeviceIdType.MESH

HD = 128
KV = 4
EXPERTS = 32
TOPK = 8
CAP = 24


EPS = 1e-06
ROPE_BASE = 1000000.0


def shifted_2(x, axis, by):
    length = lax.axis_size(axis)
    return lax.ppermute(x, axis, [(i, (i + by) % length) for i in range(length)])


def rms_scale(values, gain_row):
    mean_sq = jnp.mean(values * values, axis=-1, keepdims=True)
    return values * lax.rsqrt(mean_sq + EPS) * gain_row


def rotate(values, positions):
    half_width = values.shape[-1] // 2
    frequency = ROPE_BASE ** (-jnp.arange(half_width, dtype=jnp.float32) * 2.0 / values.shape[-1])
    angles = positions[:, None] * frequency[None, :]
    cosines = jnp.cos(angles)[:, None, :]
    sine_table = jnp.sin(angles)[:, None, :]
    leading = values[..., :half_width]
    trailing = values[..., half_width:]
    return jnp.concatenate(
        [leading * cosines - trailing * sine_table, trailing * cosines + leading * sine_table],
        axis=-1,
    )


def head_block(q_block, key_rows, value_rows, seg_block, seg_all, pos_block, pos_all, score_scale):
    scores = (
        jnp.einsum("qhd,kd->hqk", q_block, key_rows, preferred_element_type=jnp.float32)
        * score_scale
    )
    allowed = (seg_block[:, None] == seg_all[None, :]) & (pos_all[None, :] <= pos_block[:, None])
    scores = jnp.where(allowed[None], scores, -1e30)
    row_max = jnp.max(scores, axis=-1, keepdims=True)
    shifted = jnp.exp(scores - row_max)
    probability = (shifted / jnp.sum(shifted, axis=-1, keepdims=True)).astype(jnp.bfloat16)
    return jnp.einsum(
        "hqk,kd->qhd", probability, value_rows, preferred_element_type=jnp.float32
    ).astype(jnp.bfloat16)


def expert_rows(grouped, gate_up, down_proj):
    gate_up_out = jnp.einsum("necd,edf->necf", grouped, gate_up, preferred_element_type=jnp.float32)
    half_width = down_proj.shape[1]
    hidden = (jax.nn.silu(gate_up_out[..., :half_width]) * gate_up_out[..., half_width:]).astype(
        jnp.bfloat16
    )
    return jnp.einsum(
        "necf,efd->necd", hidden, down_proj, preferred_element_type=jnp.float32
    ).astype(jnp.bfloat16)


def send_back(results):
    return lax.all_to_all(results, "expert", split_axis=0, concat_axis=0, tiled=True)


def per_device_general(
    acts,
    norm_gains,
    w_query,
    w_keyval,
    w_out,
    w_gate_up,
    w_down,
    expert_ids,
    gate_weights,
    segment_ids,
):
    device_count = lax.axis_size("expert")
    my_index = lax.axis_index("expert")
    tok_rows = acts.shape[1]
    width = acts.shape[2]
    head_dev = w_query.shape[2] // HD
    local_experts = w_gate_up.shape[1]
    heads_total = head_dev * device_count
    gains = norm_gains[0]
    x_wide = acts[0].astype(jnp.float32)
    normed = rms_scale(x_wide, gains[0]).astype(jnp.bfloat16)
    kv_index = my_index * head_dev // (heads_total // KV)
    query_weight = w_query[0]
    gathered_keyval = lax.all_gather(w_keyval[0], "expert", axis=0, tiled=True)
    head_keyval = lax.dynamic_index_in_dim(gathered_keyval, kv_index, 1, keepdims=False)
    row_piece = lax.all_gather(normed, "expert", axis=0, tiled=True)
    piece_rows = row_piece.shape[0]
    positions = jnp.arange(piece_rows).astype(jnp.float32)
    query_piece_rows = row_piece.shape[0]
    query_positions = jnp.arange(query_piece_rows).astype(jnp.float32)
    queries = jnp.dot(row_piece, query_weight, preferred_element_type=jnp.float32).reshape(
        query_piece_rows, head_dev, HD
    )
    queries = (
        rotate(queries, query_positions)
        .astype(jnp.bfloat16)
        .reshape(query_piece_rows, head_dev * HD)
    )
    keyval = jnp.dot(row_piece, head_keyval, preferred_element_type=jnp.float32)
    key_rows = rotate(keyval[:, None, :HD], positions).astype(jnp.bfloat16).reshape(piece_rows, HD)
    value_rows = keyval[:, HD:].astype(jnp.bfloat16)
    projected = jnp.concatenate([queries, key_rows, value_rows], axis=1)
    tokens = projected.shape[0]
    all_queries = projected[:, : head_dev * HD].reshape(tokens, head_dev, HD)
    all_keys = projected[:, head_dev * HD : (head_dev + 1) * HD]
    all_values = projected[:, (head_dev + 1) * HD :]
    segments = segment_ids[0]
    all_positions = jnp.arange(tokens)
    q_rows = min(512, tokens)
    score_scale = 1.0 / math.sqrt(HD)

    def attend(first_row):
        q_block = lax.dynamic_slice_in_dim(all_queries, first_row, q_rows, 0)
        seg_block = lax.dynamic_slice_in_dim(segments, first_row, q_rows, 0)
        pos_block = first_row + jnp.arange(q_rows)
        return head_block(
            q_block,
            all_keys,
            all_values,
            seg_block,
            segments,
            pos_block,
            all_positions,
            score_scale,
        )

    block_starts = jnp.arange(tokens // q_rows) * q_rows
    attended = lax.map(attend, block_starts).reshape(tokens, head_dev * HD)
    out_weight = w_out[0]
    attention = lax.psum_scatter(
        jnp.dot(attended, out_weight, preferred_element_type=jnp.float32).astype(jnp.bfloat16),
        "expert",
        scatter_dimension=0,
        tiled=True,
    ).astype(jnp.float32)
    middle_wide = (x_wide + attention).astype(jnp.bfloat16).astype(jnp.float32)
    mixer_in = rms_scale(middle_wide, gains[1]).astype(jnp.bfloat16)
    routes_flat = expert_ids[0].reshape(-1)
    onehot = (routes_flat[:, None] == jnp.arange(EXPERTS, dtype=jnp.int32)[None, :]).astype(
        jnp.int32
    )
    earlier = jnp.cumsum(onehot, axis=0) - onehot
    slot_rank = jnp.sum(earlier * onehot, axis=1)
    slot_index = routes_flat * CAP + slot_rank
    routed = jnp.repeat(mixer_in, TOPK, axis=0)
    send_rows = (
        jnp.zeros((EXPERTS * CAP, width), jnp.bfloat16)
        .at[slot_index]
        .set(routed)
        .reshape(EXPERTS, CAP, width)
    )
    gate_up = w_gate_up[0]
    down_proj = w_down[0]
    received = lax.all_to_all(send_rows, "expert", split_axis=0, concat_axis=0, tiled=True)
    source_count = received.shape[0] // local_experts
    grouped = received.reshape(source_count, local_experts, received.shape[1], width)
    outputs = expert_rows(grouped, gate_up, down_proj)
    returned = send_back(outputs.reshape(received.shape))
    picked = (
        returned.reshape(EXPERTS * CAP, width)[slot_index]
        .astype(jnp.float32)
        .reshape(tok_rows, TOPK, width)
    )
    mixed = jnp.sum(picked * gate_weights[0][:, :, None], axis=1)
    result = (middle_wide + mixed).astype(jnp.bfloat16)
    handed = shifted_2(result, "section", 1)
    return handed[None]


LINE = 4
GROUP = 8


def greet(section_too):
    section, me = lax.axis_index("section"), lax.axis_index("expert")
    barrier = pltpu.get_barrier_semaphore()
    for step in range(1, GROUP):
        other = lax.rem(me + step, GROUP)
        pl.semaphore_signal(barrier, inc=1, device_id=(section, other), device_id_type=MESH)
    count = GROUP - 1
    if section_too:
        sections = lax.axis_size("section")
        for step in (1, sections - 1):
            other = lax.rem(section + step, sections)
            pl.semaphore_signal(barrier, inc=1, device_id=(other, me), device_id_type=MESH)
        count += 2
    pl.semaphore_wait(barrier, count)


def gather_line(z, rows, send_sems, recv_sems):
    section, me = lax.axis_index("section"), lax.axis_index("expert")
    x = lax.rem(me, 2)
    partner = z * 2 + 1 - x

    def copy(shard, to, way):
        return pltpu.make_async_remote_copy(
            src_ref=rows.at[shard],
            dst_ref=rows.at[shard],
            send_sem=send_sems.at[shard, way],
            recv_sem=recv_sems.at[shard],
            device_id=(section, to),
            device_id_type=MESH,
        )

    sent = []

    def send(shard, to, way):
        out = copy(shard, to, way)
        out.start()
        sent.append(out)

    own = z * 2 + x
    if z < LINE - 1:
        send(own, own + 2, 0)
    if z > 0:
        send(own, own - 2, 1)
    send(own, partner, 2)
    for far in range(1, LINE):
        if z - far >= 0:
            shard = (z - far) * 2 + x
            copy(shard, partner, 2).wait_recv()
            if z < LINE - 1:
                send(shard, own + 2, 0)
            send(shard, partner, 2)
        if z + far < LINE:
            shard = (z + far) * 2 + x
            copy(shard, partner, 2).wait_recv()
            if z > 0:
                send(shard, own - 2, 1)
            send(shard, partner, 2)

    def finish():
        for place in range(LINE):
            copy(place * 2 + 1 - x, partner, 2).wait_recv()
        for out in sent:
            out.wait_send()

    return finish


LINE_ORDER = ((3, 2, 1, 0), (3, 0, 2, 1), (0, 3, 1, 2), (0, 1, 2, 3))


def scatter_line(z, terms, from_pair, from_below, from_above, outgoing, pair_send, pair_recv,
                 line_send, below_recv, above_recv, total):
    section, me = lax.axis_index("section"), lax.axis_index("expert")
    x = lax.rem(me, 2)
    own = z * 2 + x
    partner = z * 2 + 1 - x
    pair_copies = {}
    for place in LINE_ORDER[z]:
        pair_copies[place] = pltpu.make_async_remote_copy(
            src_ref=terms.at[place * 2 + 1 - x],
            dst_ref=from_pair.at[place],
            send_sem=pair_send.at[place],
            recv_sem=pair_recv.at[place],
            device_id=(section, partner),
            device_id_type=MESH,
        )
        pair_copies[place].start()

    def line_copy(place, up):
        return pltpu.make_async_remote_copy(
            src_ref=outgoing.at[place],
            dst_ref=(from_below if up else from_above).at[place],
            send_sem=line_send.at[place],
            recv_sem=(below_recv if up else above_recv).at[place],
            device_id=(section, own + 2 if up else own - 2),
            device_id_type=MESH,
        )

    sent = []
    for place in LINE_ORDER[z]:
        pair_copies[place].wait_recv()
        parts = [terms.at[place * 2 + x], from_pair.at[place]]
        if place >= z and z > 0:
            line_copy(place, True).wait_recv()
            parts.append(from_below.at[place])
        if place <= z and z < LINE - 1:
            line_copy(place, False).wait_recv()
            parts.append(from_above.at[place])
        value = parts[0][...].astype(jnp.float32)
        for part in parts[1:]:
            value = value + part[...].astype(jnp.float32)
        if place == z:
            total[...] = value
        else:
            outgoing[place] = value.astype(jnp.bfloat16)
            out = line_copy(place, place > z)
            out.start()
            sent.append(out)
    for place in range(LINE):
        pair_copies[place].wait_send()
    for out in sent:
        out.wait_send()


def scatter_scratch(rows, width):
    slots = pltpu.VMEM((LINE, rows, width), jnp.bfloat16)
    sems = pltpu.SemaphoreType.DMA((LINE,))
    return [slots] * 4 + [sems] * 5 + [pltpu.VMEM((rows, width), jnp.float32)]


def opening_kernel(acts, gains, keyval, routes, rows, weights, all_routes,
                   send_sems, recv_sems, keyval_send, keyval_recv, route_send, route_recv,
                   local_sem):
    section, me = lax.axis_index("section"), lax.axis_index("expert")
    rows[me] = rms_scale(acts[...].astype(jnp.float32), gains[0:1, :]).astype(jnp.bfloat16)
    greet(False)
    place = me // 2
    own_weights = pltpu.make_async_copy(keyval.at[place], weights.at[me], local_sem.at[0])
    own_routes = pltpu.make_async_copy(routes, all_routes.at[me], local_sem.at[1])

    def side_copies():
        keyval_copies, route_copies = [], []
        for step in range(1, GROUP):
            other = lax.rem(me + step, GROUP)
            keyval_copies.append(pltpu.make_async_remote_copy(
                src_ref=keyval.at[other // 2],
                dst_ref=weights.at[me],
                send_sem=keyval_send.at[step],
                recv_sem=keyval_recv.at[step],
                device_id=(section, other),
                device_id_type=MESH,
            ))
            route_copies.append(pltpu.make_async_remote_copy(
                src_ref=routes,
                dst_ref=all_routes.at[me],
                send_sem=route_send.at[step],
                recv_sem=route_recv.at[step],
                device_id=(section, other),
                device_id_type=MESH,
            ))
        return keyval_copies + route_copies

    side = side_copies()
    own_weights.start()
    own_routes.start()
    for out in side:
        out.start()
    for z in range(LINE):

        @pl.when(place == z)
        def _(z=z):
            gather_line(z, rows, send_sems, recv_sems)()

    for out in side:
        out.wait_recv()
    for out in side:
        out.wait_send()
    own_weights.wait()
    own_routes.wait()


def turning_kernel(terms, acts, gains, rows, middle,
                   from_pair, from_below, from_above, outgoing, pair_send, pair_recv,
                   line_send, below_recv, above_recv, total, send_sems, recv_sems):
    me = lax.axis_index("expert")
    greet(False)
    for z in range(LINE):

        @pl.when(me // 2 == z)
        def _(z=z):
            scatter_line(z, terms, from_pair, from_below, from_above, outgoing, pair_send,
                         pair_recv, line_send, below_recv, above_recv, total)
            joined = (acts[...].astype(jnp.float32) + total[...]).astype(jnp.bfloat16)
            middle[...] = joined
            rows[me] = rms_scale(joined.astype(jnp.float32), gains[1:2, :]).astype(jnp.bfloat16)
            gather_line(z, rows, send_sems, recv_sems)()


def closing_kernel(terms, middle, handed,
                   from_pair, from_below, from_above, outgoing, pair_send, pair_recv,
                   line_send, below_recv, above_recv, total, result, hand_send, hand_recv):
    section, me = lax.axis_index("section"), lax.axis_index("expert")
    greet(True)
    for z in range(LINE):

        @pl.when(me // 2 == z)
        def _(z=z):
            scatter_line(z, terms, from_pair, from_below, from_above, outgoing, pair_send,
                         pair_recv, line_send, below_recv, above_recv, total)

    result[...] = (middle[...].astype(jnp.float32) + total[...]).astype(jnp.bfloat16)
    hand = pltpu.make_async_remote_copy(
        src_ref=result,
        dst_ref=handed,
        send_sem=hand_send,
        recv_sem=hand_recv,
        device_id=(lax.rem(section + 1, lax.axis_size("section")), me),
        device_id_type=MESH,
    )
    hand.start()
    hand.wait()


def in_vmem(count):
    return [pl.BlockSpec(memory_space=pltpu.VMEM)] * count


def remote_params(collective_id):
    return pltpu.CompilerParams(
        collective_id=collective_id, has_side_effects=True, vmem_limit_bytes=40 << 20
    )


def per_device(
    acts,
    norm_gains,
    w_query,
    w_keyval,
    w_out,
    w_gate_up,
    w_down,
    expert_ids,
    gate_weights,
    segment_ids,
):
    my_index = lax.axis_index("expert")
    tok_rows, width = acts.shape[1:]
    head_dev = w_query.shape[2] // HD
    local_experts = w_gate_up.shape[1]
    gains = norm_gains[0]
    tokens = tok_rows * GROUP
    keyval = w_keyval[0].transpose(1, 0, 2)
    keyval_rows = keyval.shape[1]
    pairs = tok_rows * TOPK
    routes = jnp.concatenate(
        [expert_ids[0].astype(jnp.float32).reshape(-1, 128), gate_weights[0].reshape(-1, 128)]
    )
    dma = pltpu.SemaphoreType.DMA
    row_piece, head_keyval, all_routes = pl.pallas_call(
        opening_kernel,
        out_shape=[
            jax.ShapeDtypeStruct((GROUP, tok_rows, width), jnp.bfloat16),
            jax.ShapeDtypeStruct((GROUP, keyval_rows, 2 * HD), jnp.bfloat16),
            jax.ShapeDtypeStruct((GROUP,) + routes.shape, jnp.float32),
        ],
        in_specs=in_vmem(4),
        out_specs=in_vmem(3),
        scratch_shapes=[
            dma((GROUP, 3)), dma((GROUP,)), dma((GROUP,)), dma((GROUP,)), dma((GROUP,)),
            dma((GROUP,)), dma((2,)),
        ],
        compiler_params=remote_params(0),
    )(acts[0], gains, keyval, routes)
    row_piece = row_piece.reshape(tokens, width)
    head_keyval = head_keyval.reshape(width, 2 * HD)

    positions = jnp.arange(tokens).astype(jnp.float32)
    queries = jnp.dot(row_piece, w_query[0], preferred_element_type=jnp.float32)
    queries = rotate(queries.reshape(tokens, head_dev, HD), positions).astype(jnp.bfloat16)
    keyval_out = jnp.dot(row_piece, head_keyval, preferred_element_type=jnp.float32)
    key_rows = rotate(keyval_out[:, None, :HD], positions).astype(jnp.bfloat16).reshape(tokens, HD)
    value_rows = keyval_out[:, HD:].astype(jnp.bfloat16)
    segments = segment_ids[0]
    token_order = jnp.arange(tokens)
    attended = head_block(
        queries, key_rows, value_rows, segments, segments, token_order, token_order,
        1.0 / math.sqrt(HD),
    ).reshape(tokens, head_dev * HD)
    terms = jnp.dot(attended, w_out[0], preferred_element_type=jnp.float32).astype(jnp.bfloat16)
    mixer_rows, middle = pl.pallas_call(
        turning_kernel,
        out_shape=[
            jax.ShapeDtypeStruct((GROUP, tok_rows, width), jnp.bfloat16),
            jax.ShapeDtypeStruct((tok_rows, width), jnp.bfloat16),
        ],
        in_specs=in_vmem(3),
        out_specs=in_vmem(2),
        scratch_shapes=scatter_scratch(tok_rows, width) + [dma((GROUP, 3)), dma((GROUP,))],
        compiler_params=remote_params(1),
    )(terms.reshape(GROUP, tok_rows, width), acts[0], gains)
    mixer_rows = mixer_rows.reshape(tokens, width)

    lines = pairs // 128
    all_ids = all_routes[:, :lines].reshape(tokens, TOPK).astype(jnp.int32)
    all_gates = all_routes[:, lines:].reshape(tokens, TOPK)
    experts_here = my_index * local_experts + jnp.arange(local_experts, dtype=jnp.int32)
    named = all_ids[:, :, None] == experts_here[None, None, :]
    gates = jnp.sum(jnp.where(named, all_gates[:, :, None], 0.0), axis=1)
    member = jnp.any(named, axis=1)
    before = (token_order[:, None] > token_order[None, :]).astype(jnp.bfloat16)
    rank = jnp.dot(before, member.astype(jnp.bfloat16), preferred_element_type=jnp.float32)
    slots = GROUP * CAP
    slot_of = jnp.where(member, rank.astype(jnp.int32), -1).T
    chosen = slot_of[:, None, :] == jnp.arange(slots, dtype=jnp.int32)[None, :, None]
    slot_gates = jnp.sum(jnp.where(chosen, gates.T[:, None, :], 0.0), axis=2)
    chosen = chosen.astype(jnp.bfloat16)
    grouped = jnp.einsum(
        "est,td->esd", chosen, mixer_rows, preferred_element_type=jnp.float32
    ).astype(jnp.bfloat16)
    gate_up_out = jnp.einsum(
        "esd,edf->esf", grouped, w_gate_up[0], preferred_element_type=jnp.float32
    )
    ff = w_down.shape[2]
    hidden = (jax.nn.silu(gate_up_out[..., :ff]) * gate_up_out[..., ff:]).astype(jnp.bfloat16)
    outputs = jnp.einsum("esf,efd->esd", hidden, w_down[0], preferred_element_type=jnp.float32)
    outputs = (outputs * slot_gates[:, :, None]).astype(jnp.bfloat16)
    mixed = jnp.dot(
        chosen.reshape(local_experts * slots, tokens).T,
        outputs.reshape(local_experts * slots, width),
        preferred_element_type=jnp.float32,
    ).astype(jnp.bfloat16)

    handed = pl.pallas_call(
        closing_kernel,
        out_shape=jax.ShapeDtypeStruct((tok_rows, width), jnp.bfloat16),
        in_specs=in_vmem(2),
        out_specs=pl.BlockSpec(memory_space=pltpu.VMEM),
        scratch_shapes=scatter_scratch(tok_rows, width)
        + [pltpu.VMEM((tok_rows, width), jnp.bfloat16), dma, dma],
        compiler_params=remote_params(2),
    )(mixed.reshape(GROUP, tok_rows, width), middle)
    return handed[None]


def solution(mesh):
    placed = (
        P("section", "expert", None),
        P("section", None, None),
        P("section", None, "expert"),
        P("section", "expert", None, None),
        P("section", "expert", None),
        P("section", "expert", None, None),
        P("section", "expert", None, None),
        P("section", "expert", None),
        P("section", "expert", None),
        P("section", None),
    )
    return jax.shard_map(
        per_device if mesh.shape["expert"] == GROUP else per_device_general,
        mesh=mesh,
        in_specs=placed,
        out_specs=P("section", "expert", None),
        check_vma=False,
    )
```

```python
import functools
import math

import jax
import jax.numpy as jnp
from jax import lax
from jax.experimental import pallas as pl
from jax.experimental.pallas import tpu as pltpu
from jax.sharding import PartitionSpec as P

MESH = pl.DeviceIdType.MESH

HD = 128
KV = 4
EXPERTS = 32
TOPK = 8
CAP = 24


EPS = 1e-06
ROPE_BASE = 1000000.0


def shifted_2(x, axis, by):
    length = lax.axis_size(axis)
    return lax.ppermute(x, axis, [(i, (i + by) % length) for i in range(length)])


def rms_scale(values, gain_row):
    mean_sq = jnp.mean(values * values, axis=-1, keepdims=True)
    return values * lax.rsqrt(mean_sq + EPS) * gain_row


def rotate(values, positions):
    half_width = values.shape[-1] // 2
    frequency = ROPE_BASE ** (-jnp.arange(half_width, dtype=jnp.float32) * 2.0 / values.shape[-1])
    angles = positions[:, None] * frequency[None, :]
    cosines = jnp.cos(angles)[:, None, :]
    sine_table = jnp.sin(angles)[:, None, :]
    leading = values[..., :half_width]
    trailing = values[..., half_width:]
    return jnp.concatenate(
        [leading * cosines - trailing * sine_table, trailing * cosines + leading * sine_table],
        axis=-1,
    )


def head_block(q_block, key_rows, value_rows, seg_block, seg_all, pos_block, pos_all, score_scale):
    scores = (
        jnp.einsum("qhd,kd->hqk", q_block, key_rows, preferred_element_type=jnp.float32)
        * score_scale
    )
    allowed = (seg_block[:, None] == seg_all[None, :]) & (pos_all[None, :] <= pos_block[:, None])
    scores = jnp.where(allowed[None], scores, -1e30)
    row_max = jnp.max(scores, axis=-1, keepdims=True)
    shifted = jnp.exp(scores - row_max)
    probability = (shifted / jnp.sum(shifted, axis=-1, keepdims=True)).astype(jnp.bfloat16)
    return jnp.einsum(
        "hqk,kd->qhd", probability, value_rows, preferred_element_type=jnp.float32
    ).astype(jnp.bfloat16)


def expert_rows(grouped, gate_up, down_proj):
    gate_up_out = jnp.einsum("necd,edf->necf", grouped, gate_up, preferred_element_type=jnp.float32)
    half_width = down_proj.shape[1]
    hidden = (jax.nn.silu(gate_up_out[..., :half_width]) * gate_up_out[..., half_width:]).astype(
        jnp.bfloat16
    )
    return jnp.einsum(
        "necf,efd->necd", hidden, down_proj, preferred_element_type=jnp.float32
    ).astype(jnp.bfloat16)


def send_back(results):
    return lax.all_to_all(results, "expert", split_axis=0, concat_axis=0, tiled=True)


def per_device_general(
    acts,
    norm_gains,
    w_query,
    w_keyval,
    w_out,
    w_gate_up,
    w_down,
    expert_ids,
    gate_weights,
    segment_ids,
):
    device_count = lax.axis_size("expert")
    my_index = lax.axis_index("expert")
    tok_rows = acts.shape[1]
    width = acts.shape[2]
    head_dev = w_query.shape[2] // HD
    local_experts = w_gate_up.shape[1]
    heads_total = head_dev * device_count
    gains = norm_gains[0]
    x_wide = acts[0].astype(jnp.float32)
    normed = rms_scale(x_wide, gains[0]).astype(jnp.bfloat16)
    kv_index = my_index * head_dev // (heads_total // KV)
    query_weight = w_query[0]
    gathered_keyval = lax.all_gather(w_keyval[0], "expert", axis=0, tiled=True)
    head_keyval = lax.dynamic_index_in_dim(gathered_keyval, kv_index, 1, keepdims=False)
    row_piece = lax.all_gather(normed, "expert", axis=0, tiled=True)
    piece_rows = row_piece.shape[0]
    positions = jnp.arange(piece_rows).astype(jnp.float32)
    query_piece_rows = row_piece.shape[0]
    query_positions = jnp.arange(query_piece_rows).astype(jnp.float32)
    queries = jnp.dot(row_piece, query_weight, preferred_element_type=jnp.float32).reshape(
        query_piece_rows, head_dev, HD
    )
    queries = (
        rotate(queries, query_positions)
        .astype(jnp.bfloat16)
        .reshape(query_piece_rows, head_dev * HD)
    )
    keyval = jnp.dot(row_piece, head_keyval, preferred_element_type=jnp.float32)
    key_rows = rotate(keyval[:, None, :HD], positions).astype(jnp.bfloat16).reshape(piece_rows, HD)
    value_rows = keyval[:, HD:].astype(jnp.bfloat16)
    projected = jnp.concatenate([queries, key_rows, value_rows], axis=1)
    tokens = projected.shape[0]
    all_queries = projected[:, : head_dev * HD].reshape(tokens, head_dev, HD)
    all_keys = projected[:, head_dev * HD : (head_dev + 1) * HD]
    all_values = projected[:, (head_dev + 1) * HD :]
    segments = segment_ids[0]
    all_positions = jnp.arange(tokens)
    q_rows = min(512, tokens)
    score_scale = 1.0 / math.sqrt(HD)

    def attend(first_row):
        q_block = lax.dynamic_slice_in_dim(all_queries, first_row, q_rows, 0)
        seg_block = lax.dynamic_slice_in_dim(segments, first_row, q_rows, 0)
        pos_block = first_row + jnp.arange(q_rows)
        return head_block(
            q_block,
            all_keys,
            all_values,
            seg_block,
            segments,
            pos_block,
            all_positions,
            score_scale,
        )

    block_starts = jnp.arange(tokens // q_rows) * q_rows
    attended = lax.map(attend, block_starts).reshape(tokens, head_dev * HD)
    out_weight = w_out[0]
    attention = lax.psum_scatter(
        jnp.dot(attended, out_weight, preferred_element_type=jnp.float32).astype(jnp.bfloat16),
        "expert",
        scatter_dimension=0,
        tiled=True,
    ).astype(jnp.float32)
    middle_wide = (x_wide + attention).astype(jnp.bfloat16).astype(jnp.float32)
    mixer_in = rms_scale(middle_wide, gains[1]).astype(jnp.bfloat16)
    routes_flat = expert_ids[0].reshape(-1)
    onehot = (routes_flat[:, None] == jnp.arange(EXPERTS, dtype=jnp.int32)[None, :]).astype(
        jnp.int32
    )
    earlier = jnp.cumsum(onehot, axis=0) - onehot
    slot_rank = jnp.sum(earlier * onehot, axis=1)
    slot_index = routes_flat * CAP + slot_rank
    routed = jnp.repeat(mixer_in, TOPK, axis=0)
    send_rows = (
        jnp.zeros((EXPERTS * CAP, width), jnp.bfloat16)
        .at[slot_index]
        .set(routed)
        .reshape(EXPERTS, CAP, width)
    )
    gate_up = w_gate_up[0]
    down_proj = w_down[0]
    received = lax.all_to_all(send_rows, "expert", split_axis=0, concat_axis=0, tiled=True)
    source_count = received.shape[0] // local_experts
    grouped = received.reshape(source_count, local_experts, received.shape[1], width)
    outputs = expert_rows(grouped, gate_up, down_proj)
    returned = send_back(outputs.reshape(received.shape))
    picked = (
        returned.reshape(EXPERTS * CAP, width)[slot_index]
        .astype(jnp.float32)
        .reshape(tok_rows, TOPK, width)
    )
    mixed = jnp.sum(picked * gate_weights[0][:, :, None], axis=1)
    result = (middle_wide + mixed).astype(jnp.bfloat16)
    handed = shifted_2(result, "section", 1)
    return handed[None]


LINE = 4
GROUP = 8
CHUNKS = 4


def remote(src, dst, send_sem, recv_sem, expert, section=None):
    if section is None:
        section = lax.axis_index("section")
    return pltpu.make_async_remote_copy(
        src_ref=src,
        dst_ref=dst,
        send_sem=send_sem,
        recv_sem=recv_sem,
        device_id=(section, expert),
        device_id_type=MESH,
    )


def greet(section_too):
    section, me = lax.axis_index("section"), lax.axis_index("expert")
    barrier = pltpu.get_barrier_semaphore()
    for step in range(1, GROUP):
        other = lax.rem(me + step, GROUP)
        pl.semaphore_signal(barrier, inc=1, device_id=(section, other), device_id_type=MESH)
    count = GROUP - 1
    if section_too:
        sections = lax.axis_size("section")
        for step in (1, sections - 1):
            other = lax.rem(section + step, sections)
            pl.semaphore_signal(barrier, inc=1, device_id=(other, me), device_id_type=MESH)
        count += 2
    pl.semaphore_wait(barrier, count)


def at_place(body):
    me = lax.axis_index("expert")
    x = lax.rem(me, 2)
    for z in range(LINE):

        @pl.when(me // 2 == z)
        def _(z=z):
            body(z, x, z * 2 + x, z * 2 + 1 - x)


class Gather:
    def __init__(self, rows, send_sems, recv_sems):
        self.rows, self.send_sems, self.recv_sems = rows, send_sems, recv_sems

    def copy(self, chunk, shard, to, way):
        return remote(
            self.rows.at[chunk, shard], self.rows.at[chunk, shard],
            self.send_sems.at[chunk, shard, way], self.recv_sems.at[chunk, shard], to,
        )

    def first(self, chunk, z, own, partner):
        out = []
        if z < LINE - 1:
            out.append(self.copy(chunk, own, own + 2, 0))
        if z > 0:
            out.append(self.copy(chunk, own, own - 2, 1))
        return out + [self.copy(chunk, own, partner, 2)]

    def passing(self, chunk, z, x, own, partner):
        out = []
        for far in range(1, LINE):
            if z - far >= 0:
                shard = (z - far) * 2 + x
                onward = [self.copy(chunk, shard, own + 2, 0)] if z < LINE - 1 else []
                out.append((shard, onward + [self.copy(chunk, shard, partner, 2)]))
            if z + far < LINE:
                shard = (z + far) * 2 + x
                onward = [self.copy(chunk, shard, own - 2, 1)] if z > 0 else []
                out.append((shard, onward + [self.copy(chunk, shard, partner, 2)]))
        return out

    def start(self, chunk, z, x, own, partner):
        for out in self.first(chunk, z, own, partner):
            out.start()

    def forward(self, chunk, z, x, own, partner):
        for shard, onward in self.passing(chunk, z, x, own, partner):
            self.copy(chunk, shard, partner, 2).wait_recv()
            for out in onward:
                out.start()

    def arrive(self, chunk, z, x, own, partner):
        for place in range(LINE):
            self.copy(chunk, place * 2 + 1 - x, partner, 2).wait_recv()

    def drain(self, chunk, z, x, own, partner):
        for out in self.first(chunk, z, own, partner):
            out.wait_send()
        for _, onward in self.passing(chunk, z, x, own, partner):
            for out in onward:
                out.wait_send()


LINE_ORDER = ((3, 2, 1, 0), (3, 0, 2, 1), (0, 3, 1, 2), (0, 1, 2, 3))


class Scatter:
    def __init__(self, terms, total, from_pair, from_below, from_above, outgoing, pair_send,
                 pair_recv, line_send, below_recv, above_recv):
        self.terms, self.total = terms, total
        self.from_pair, self.from_below, self.from_above = from_pair, from_below, from_above
        self.outgoing = outgoing
        self.pair_send, self.pair_recv = pair_send, pair_recv
        self.line_send, self.below_recv, self.above_recv = line_send, below_recv, above_recv

    def pair_copy(self, chunk, place, x, partner):
        return remote(
            self.terms.at[chunk, place * 2 + 1 - x], self.from_pair.at[chunk, place],
            self.pair_send.at[chunk, place], self.pair_recv.at[chunk, place], partner,
        )

    def line_copy(self, chunk, place, up, own):
        landing, sems = (
            (self.from_below, self.below_recv) if up else (self.from_above, self.above_recv)
        )
        return remote(
            self.outgoing.at[chunk, place], landing.at[chunk, place],
            self.line_send.at[chunk, place], sems.at[chunk, place],
            own + 2 if up else own - 2,
        )

    def start(self, chunk, z, x, own, partner):
        for place in LINE_ORDER[z]:
            self.pair_copy(chunk, place, x, partner).start()

    def reduce(self, chunk, z, x, own, partner):
        for place in LINE_ORDER[z]:
            self.pair_copy(chunk, place, x, partner).wait_recv()
            parts = [self.from_pair.at[chunk, place]]
            if place >= z and z > 0:
                self.line_copy(chunk, place, True, own).wait_recv()
                parts.append(self.from_below.at[chunk, place])
            if place <= z and z < LINE - 1:
                self.line_copy(chunk, place, False, own).wait_recv()
                parts.append(self.from_above.at[chunk, place])
            value = self.terms[chunk, place * 2 + x].astype(jnp.float32)
            for part in parts:
                value = value + part[...].astype(jnp.float32)
            if place == z:
                self.total[chunk] = value
            else:
                self.outgoing[chunk, place] = value.astype(jnp.bfloat16)
                self.line_copy(chunk, place, place > z, own).start()

    def drain(self, chunk, z, x, own, partner):
        for place in range(LINE):
            self.pair_copy(chunk, place, x, partner).wait_send()
            if place != z:
                self.line_copy(chunk, place, place > z, own).wait_send()


def scatter_scratch(rows, columns):
    slots = pltpu.VMEM((CHUNKS, LINE, rows, columns), jnp.bfloat16)
    sems = pltpu.SemaphoreType.DMA((CHUNKS, LINE))
    return [slots] * 4 + [sems] * 5


def opening_kernel(acts, gains, keyval, gates, rows, weights, all_gates,
                   send_sems, recv_sems, keyval_send, keyval_recv, pass_send, gate_send,
                   gate_recv, local_sem):
    section, me = lax.axis_index("section"), lax.axis_index("expert")
    rows[0, me] = rms_scale(acts[...].astype(jnp.float32), gains[0:1, :]).astype(jnp.bfloat16)
    greet(False)
    gather = Gather(rows, send_sems, recv_sems)
    own_gates = pltpu.make_async_copy(gates.at[me], all_gates.at[me], local_sem.at[1])
    own_weights = pltpu.make_async_copy(keyval.at[me // 2], weights.at[me], local_sem.at[0])
    gate_copies = []
    for step in range(1, GROUP):
        other = lax.rem(me + step, GROUP)
        gate_copies.append(
            remote(gates.at[other], all_gates.at[me], gate_send.at[step], gate_recv.at[step], other)
        )

    def line_weights(place, z, own):
        return remote(
            keyval.at[place], weights.at[own], keyval_send.at[place], keyval_recv.at[own],
            own + 2 * (place - z),
        )

    def pass_weights(place, z, x, partner):
        shard = place * 2 + x
        source = keyval.at[z] if place == z else weights.at[shard]
        return remote(source, weights.at[shard], pass_send.at[place], keyval_recv.at[shard], partner)

    def begin(z, x, own, partner):
        gather.start(0, z, x, own, partner)
        for place in LINE_ORDER[z]:
            if place != z:
                line_weights(place, z, own).start()
        pass_weights(z, z, x, partner).start()

    def through(z, x, own, partner):
        nearest = sorted((p for p in range(LINE) if p != z), key=lambda p: abs(p - z))
        for place, (shard, onward) in zip(nearest, gather.passing(0, z, x, own, partner)):
            gather.copy(0, shard, partner, 2).wait_recv()
            for out in onward:
                out.start()
            source = place * 2 + x
            remote(
                weights.at[source], weights.at[source], pass_send.at[place],
                keyval_recv.at[source], partner,
            ).wait_recv()
            pass_weights(place, z, x, partner).start()
        gather.arrive(0, z, x, own, partner)
        for place in range(LINE):
            source = place * 2 + 1 - x
            remote(
                weights.at[source], weights.at[source], pass_send.at[place],
                keyval_recv.at[source], partner,
            ).wait_recv()
        gather.drain(0, z, x, own, partner)
        for place in range(LINE):
            if place != z:
                line_weights(place, z, own).wait_send()
            pass_weights(place, z, x, partner).wait_send()

    at_place(begin)
    own_weights.start()
    own_gates.start()
    for out in gate_copies:
        out.start()
    at_place(through)
    for out in gate_copies:
        out.wait_recv()
    for out in gate_copies:
        out.wait_send()
    own_weights.wait()
    own_gates.wait()


def closing_kernel(terms, acts, gains, chosen, chosen_t, slot_gates, w_gate_up, w_down, handed,
                   gate_up, down, work, rows, middle, hidden_sums, hidden, scaled, total, result,
                   *more):
    first_scratch, more = more[:9], more[9:]
    last_scratch, more = more[:9], more[9:]
    send_sems, recv_sems, work_sems, up_sems, down_sems, hand_send, hand_recv = more
    section, me = lax.axis_index("section"), lax.axis_index("expert")
    columns = work.shape[-1]
    tok_rows = work.shape[-2]
    tokens = GROUP * tok_rows
    local_experts = gate_up.shape[0]
    ff = hidden.shape[-1]
    first = Scatter(work, total, *first_scratch)
    last = Scatter(work, total, *last_scratch)
    gather = Gather(rows, send_sems, recv_sems)

    def part(chunk):
        return pl.ds(chunk * columns, columns)

    loads = [
        pltpu.make_async_copy(terms.at[:, :, part(c)], work.at[c], work_sems.at[c])
        for c in range(CHUNKS)
    ]
    up_loads = [
        pltpu.make_async_copy(w_gate_up.at[:, part(c), :], gate_up.at[:, part(c), :], up_sems.at[c])
        for c in range(CHUNKS)
    ]
    down_loads = [
        pltpu.make_async_copy(w_down.at[:, :, part(c)], down.at[c % 2], down_sems.at[c % 2])
        for c in range(CHUNKS)
    ]
    for load in loads:
        load.start()
    for load in up_loads + down_loads[:2]:
        load.start()
    greet(True)
    for c in range(CHUNKS):
        loads[c].wait()
        at_place(functools.partial(first.start, c))

    def first_sums(z, x, own, partner):
        for c in range(CHUNKS):
            first.reduce(c, z, x, own, partner)
        for c in range(CHUNKS):
            first.drain(c, z, x, own, partner)

    at_place(first_sums)
    squares = jnp.zeros((tok_rows, 1), jnp.float32)
    for c in range(CHUNKS):
        joined = (acts[:, part(c)].astype(jnp.float32) + total[c]).astype(jnp.bfloat16)
        middle[c] = joined
        wide = joined.astype(jnp.float32)
        squares = squares + jnp.sum(wide * wide, axis=-1, keepdims=True)
    scale = lax.rsqrt(squares / (CHUNKS * columns) + EPS)
    for c in range(CHUNKS):
        rows[c, me] = (middle[c].astype(jnp.float32) * scale * gains[1:2, part(c)]).astype(
            jnp.bfloat16
        )
        at_place(functools.partial(gather.start, c))

    def gate_up_chunk(c):
        up_loads[c].wait()
        all_rows = rows[c].reshape(tokens, columns)

        @pl.loop(0, local_experts)
        def _(e):
            grouped = jnp.dot(chosen[e], all_rows, preferred_element_type=jnp.float32)
            product = jnp.dot(
                grouped.astype(jnp.bfloat16), gate_up[e, part(c), :],
                preferred_element_type=jnp.float32,
            )
            if c == 0:
                hidden_sums[e] = product
            else:
                hidden_sums[e] += product

    at_place(functools.partial(gather.forward, 0))
    for c in range(CHUNKS):
        if c + 1 < CHUNKS:
            at_place(functools.partial(gather.forward, c + 1))
        at_place(functools.partial(gather.arrive, c))
        gate_up_chunk(c)

    @pl.loop(0, local_experts)
    def _(e):
        gate = hidden_sums[e, :, :ff]
        hidden[e] = (gate / (1.0 + jnp.exp(-gate)) * hidden_sums[e, :, ff:]).astype(jnp.bfloat16)

    slots = hidden.shape[1]

    def down_chunk(c):
        down_loads[c].wait()

        @pl.loop(0, local_experts)
        def _(e):
            out = jnp.dot(hidden[e], down[c % 2, e], preferred_element_type=jnp.float32)
            scaled[pl.ds(pl.multiple_of(e * slots, slots), slots), :] = (
                out * slot_gates[e]
            ).astype(jnp.bfloat16)

        if c + 2 < CHUNKS:
            down_loads[c + 2].start()

        @pl.loop(0, GROUP)
        def _(block):
            work[c, block] = jnp.dot(
                chosen_t[block], scaled[...], preferred_element_type=jnp.float32
            ).astype(jnp.bfloat16)

        at_place(functools.partial(last.start, c))

    def hand(c):
        return remote(
            result.at[:, part(c)], handed.at[:, part(c)], hand_send.at[c], hand_recv.at[c],
            me, lax.rem(section + 1, lax.axis_size("section")),
        )

    def last_sums(c):
        at_place(functools.partial(last.reduce, c))
        result[:, part(c)] = (middle[c].astype(jnp.float32) + total[c]).astype(jnp.bfloat16)
        hand(c).start()

    down_chunk(0)
    for c in range(CHUNKS):
        if c + 1 < CHUNKS:
            down_chunk(c + 1)
        last_sums(c)

    def drain(z, x, own, partner):
        for c in range(CHUNKS):
            gather.drain(c, z, x, own, partner)
            last.drain(c, z, x, own, partner)

    at_place(drain)
    for c in range(CHUNKS):
        hand(c).wait()


def in_vmem(count):
    return [pl.BlockSpec(memory_space=pltpu.VMEM)] * count


def remote_params(collective_id, mebibytes):
    return pltpu.CompilerParams(
        collective_id=collective_id, has_side_effects=True, vmem_limit_bytes=mebibytes << 20
    )


def per_device(
    acts,
    norm_gains,
    w_query,
    w_keyval,
    w_out,
    w_gate_up,
    w_down,
    expert_ids,
    gate_weights,
    segment_ids,
):
    tok_rows, width = acts.shape[1:]
    head_dev = w_query.shape[2] // HD
    local_experts = w_gate_up.shape[1]
    gains = norm_gains[0]
    tokens = tok_rows * GROUP
    keyval = w_keyval[0].transpose(1, 0, 2)
    keyval_rows = keyval.shape[1]
    named = expert_ids[0][:, :, None] == jnp.arange(EXPERTS, dtype=jnp.int32)[None, None, :]
    dense_gates = jnp.sum(jnp.where(named, gate_weights[0][:, :, None], 0.0), axis=1)
    dense_gates = dense_gates.T.reshape(GROUP, local_experts, tok_rows)
    dma = pltpu.SemaphoreType.DMA
    row_piece, head_keyval, all_gates = pl.pallas_call(
        opening_kernel,
        out_shape=[
            jax.ShapeDtypeStruct((1, GROUP, tok_rows, width), jnp.bfloat16),
            jax.ShapeDtypeStruct((GROUP, keyval_rows, 2 * HD), jnp.bfloat16),
            jax.ShapeDtypeStruct(dense_gates.shape, jnp.float32),
        ],
        in_specs=in_vmem(4),
        out_specs=in_vmem(3),
        scratch_shapes=[
            dma((1, GROUP, 3)), dma((1, GROUP)), dma((LINE,)), dma((GROUP,)), dma((LINE,)),
            dma((GROUP,)), dma((GROUP,)), dma((2,)),
        ],
        compiler_params=remote_params(0, 40),
    )(acts[0], gains, keyval, dense_gates)
    row_piece = row_piece.reshape(tokens, width)
    head_keyval = head_keyval.reshape(width, 2 * HD)

    positions = jnp.arange(tokens).astype(jnp.float32)
    queries = jnp.dot(row_piece, w_query[0], preferred_element_type=jnp.float32)
    queries = rotate(queries.reshape(tokens, head_dev, HD), positions).astype(jnp.bfloat16)
    keyval_out = jnp.dot(row_piece, head_keyval, preferred_element_type=jnp.float32)
    key_rows = rotate(keyval_out[:, None, :HD], positions).astype(jnp.bfloat16).reshape(tokens, HD)
    value_rows = keyval_out[:, HD:].astype(jnp.bfloat16)
    segments = segment_ids[0]
    token_order = jnp.arange(tokens)
    attended = head_block(
        queries, key_rows, value_rows, segments, segments, token_order, token_order,
        1.0 / math.sqrt(HD),
    ).reshape(tokens, head_dev * HD)
    terms = jnp.dot(attended, w_out[0], preferred_element_type=jnp.float32).astype(jnp.bfloat16)

    gates = all_gates.transpose(1, 0, 2).reshape(local_experts, tokens)
    member = gates > 0
    before = (token_order[:, None] < token_order[None, :]).astype(jnp.bfloat16)
    rank = jnp.dot(member.astype(jnp.bfloat16), before, preferred_element_type=jnp.float32)
    slots = GROUP * CAP
    slot_of = jnp.where(member, rank.astype(jnp.int32), -1)
    places = jnp.arange(slots, dtype=jnp.int32)
    chosen = slot_of[:, None, :] == places[None, :, None]
    slot_gates = jnp.sum(jnp.where(chosen, gates[:, None, :], 0.0), axis=2, keepdims=True)
    chosen = chosen.astype(jnp.bfloat16)
    chosen_t = (slot_of.T[:, :, None] == places[None, None, :]).astype(jnp.bfloat16)
    chosen_t = chosen_t.reshape(GROUP, tok_rows, local_experts * slots)

    columns = width // CHUNKS
    ff = w_down.shape[2]
    vmem = pltpu.VMEM
    in_place = pl.BlockSpec(memory_space=pl.ANY)
    handed = pl.pallas_call(
        closing_kernel,
        out_shape=jax.ShapeDtypeStruct((tok_rows, width), jnp.bfloat16),
        in_specs=[in_place] + in_vmem(5) + [in_place] * 2,
        out_specs=pl.BlockSpec(memory_space=vmem),
        scratch_shapes=[
            vmem(w_gate_up.shape[1:], jnp.bfloat16),
            vmem((2, local_experts, ff, columns), jnp.bfloat16),
            vmem((CHUNKS, GROUP, tok_rows, columns), jnp.bfloat16),
            vmem((CHUNKS, GROUP, tok_rows, columns), jnp.bfloat16),
            vmem((CHUNKS, tok_rows, columns), jnp.bfloat16),
            vmem((local_experts, slots, 2 * ff), jnp.float32),
            vmem((local_experts, slots, ff), jnp.bfloat16),
            vmem((local_experts * slots, columns), jnp.bfloat16),
            vmem((CHUNKS, tok_rows, columns), jnp.float32),
            vmem((tok_rows, width), jnp.bfloat16),
        ]
        + scatter_scratch(tok_rows, columns)
        + scatter_scratch(tok_rows, columns)
        + [
            dma((CHUNKS, GROUP, 3)), dma((CHUNKS, GROUP)), dma((CHUNKS,)), dma((CHUNKS,)),
            dma((2,)), dma((CHUNKS,)), dma((CHUNKS,)),
        ],
        compiler_params=remote_params(1, 60),
    )(
        terms.reshape(GROUP, tok_rows, width), acts[0], gains, chosen, chosen_t, slot_gates,
        w_gate_up[0], w_down[0],
    )
    return handed[None]


def solution(mesh):
    placed = (
        P("section", "expert", None),
        P("section", None, None),
        P("section", None, "expert"),
        P("section", "expert", None, None),
        P("section", "expert", None),
        P("section", "expert", None, None),
        P("section", "expert", None, None),
        P("section", "expert", None),
        P("section", "expert", None),
        P("section", None),
    )
    return jax.shard_map(
        per_device if mesh.shape["expert"] == GROUP else per_device_general,
        mesh=mesh,
        in_specs=placed,
        out_specs=P("section", "expert", None),
        check_vma=False,
    )
```

```python
import math

import jax
import jax.numpy as jnp
from jax import lax
from jax.experimental import pallas as pl
from jax.experimental.pallas import tpu as pltpu
from jax.sharding import PartitionSpec as P

MESH = pl.DeviceIdType.MESH

HD = 128
KV = 4
EXPERTS = 32
TOPK = 8
CAP = 24


EPS = 1e-06
ROPE_BASE = 1000000.0


def shifted_2(x, axis, by):
    length = lax.axis_size(axis)
    return lax.ppermute(x, axis, [(i, (i + by) % length) for i in range(length)])


def rms_scale(values, gain_row):
    mean_sq = jnp.mean(values * values, axis=-1, keepdims=True)
    return values * lax.rsqrt(mean_sq + EPS) * gain_row


def rotate(values, positions):
    half_width = values.shape[-1] // 2
    frequency = ROPE_BASE ** (-jnp.arange(half_width, dtype=jnp.float32) * 2.0 / values.shape[-1])
    angles = positions[:, None] * frequency[None, :]
    cosines = jnp.cos(angles)[:, None, :]
    sine_table = jnp.sin(angles)[:, None, :]
    leading = values[..., :half_width]
    trailing = values[..., half_width:]
    return jnp.concatenate(
        [leading * cosines - trailing * sine_table, trailing * cosines + leading * sine_table],
        axis=-1,
    )


def head_block(q_block, key_rows, value_rows, seg_block, seg_all, pos_block, pos_all, score_scale):
    scores = (
        jnp.einsum("qhd,kd->hqk", q_block, key_rows, preferred_element_type=jnp.float32)
        * score_scale
    )
    allowed = (seg_block[:, None] == seg_all[None, :]) & (pos_all[None, :] <= pos_block[:, None])
    scores = jnp.where(allowed[None], scores, -1e30)
    row_max = jnp.max(scores, axis=-1, keepdims=True)
    shifted = jnp.exp(scores - row_max)
    probability = (shifted / jnp.sum(shifted, axis=-1, keepdims=True)).astype(jnp.bfloat16)
    return jnp.einsum(
        "hqk,kd->qhd", probability, value_rows, preferred_element_type=jnp.float32
    ).astype(jnp.bfloat16)


def expert_rows(grouped, gate_up, down_proj):
    gate_up_out = jnp.einsum("necd,edf->necf", grouped, gate_up, preferred_element_type=jnp.float32)
    half_width = down_proj.shape[1]
    hidden = (jax.nn.silu(gate_up_out[..., :half_width]) * gate_up_out[..., half_width:]).astype(
        jnp.bfloat16
    )
    return jnp.einsum(
        "necf,efd->necd", hidden, down_proj, preferred_element_type=jnp.float32
    ).astype(jnp.bfloat16)


def send_back(results):
    return lax.all_to_all(results, "expert", split_axis=0, concat_axis=0, tiled=True)


def per_device_general(
    acts,
    norm_gains,
    w_query,
    w_keyval,
    w_out,
    w_gate_up,
    w_down,
    expert_ids,
    gate_weights,
    segment_ids,
):
    device_count = lax.axis_size("expert")
    my_index = lax.axis_index("expert")
    tok_rows = acts.shape[1]
    width = acts.shape[2]
    head_dev = w_query.shape[2] // HD
    local_experts = w_gate_up.shape[1]
    heads_total = head_dev * device_count
    gains = norm_gains[0]
    x_wide = acts[0].astype(jnp.float32)
    normed = rms_scale(x_wide, gains[0]).astype(jnp.bfloat16)
    kv_index = my_index * head_dev // (heads_total // KV)
    query_weight = w_query[0]
    gathered_keyval = lax.all_gather(w_keyval[0], "expert", axis=0, tiled=True)
    head_keyval = lax.dynamic_index_in_dim(gathered_keyval, kv_index, 1, keepdims=False)
    row_piece = lax.all_gather(normed, "expert", axis=0, tiled=True)
    piece_rows = row_piece.shape[0]
    positions = jnp.arange(piece_rows).astype(jnp.float32)
    query_piece_rows = row_piece.shape[0]
    query_positions = jnp.arange(query_piece_rows).astype(jnp.float32)
    queries = jnp.dot(row_piece, query_weight, preferred_element_type=jnp.float32).reshape(
        query_piece_rows, head_dev, HD
    )
    queries = (
        rotate(queries, query_positions)
        .astype(jnp.bfloat16)
        .reshape(query_piece_rows, head_dev * HD)
    )
    keyval = jnp.dot(row_piece, head_keyval, preferred_element_type=jnp.float32)
    key_rows = rotate(keyval[:, None, :HD], positions).astype(jnp.bfloat16).reshape(piece_rows, HD)
    value_rows = keyval[:, HD:].astype(jnp.bfloat16)
    projected = jnp.concatenate([queries, key_rows, value_rows], axis=1)
    tokens = projected.shape[0]
    all_queries = projected[:, : head_dev * HD].reshape(tokens, head_dev, HD)
    all_keys = projected[:, head_dev * HD : (head_dev + 1) * HD]
    all_values = projected[:, (head_dev + 1) * HD :]
    segments = segment_ids[0]
    all_positions = jnp.arange(tokens)
    q_rows = min(512, tokens)
    score_scale = 1.0 / math.sqrt(HD)

    def attend(first_row):
        q_block = lax.dynamic_slice_in_dim(all_queries, first_row, q_rows, 0)
        seg_block = lax.dynamic_slice_in_dim(segments, first_row, q_rows, 0)
        pos_block = first_row + jnp.arange(q_rows)
        return head_block(
            q_block,
            all_keys,
            all_values,
            seg_block,
            segments,
            pos_block,
            all_positions,
            score_scale,
        )

    block_starts = jnp.arange(tokens // q_rows) * q_rows
    attended = lax.map(attend, block_starts).reshape(tokens, head_dev * HD)
    out_weight = w_out[0]
    attention = lax.psum_scatter(
        jnp.dot(attended, out_weight, preferred_element_type=jnp.float32).astype(jnp.bfloat16),
        "expert",
        scatter_dimension=0,
        tiled=True,
    ).astype(jnp.float32)
    middle_wide = (x_wide + attention).astype(jnp.bfloat16).astype(jnp.float32)
    mixer_in = rms_scale(middle_wide, gains[1]).astype(jnp.bfloat16)
    routes_flat = expert_ids[0].reshape(-1)
    onehot = (routes_flat[:, None] == jnp.arange(EXPERTS, dtype=jnp.int32)[None, :]).astype(
        jnp.int32
    )
    earlier = jnp.cumsum(onehot, axis=0) - onehot
    slot_rank = jnp.sum(earlier * onehot, axis=1)
    slot_index = routes_flat * CAP + slot_rank
    routed = jnp.repeat(mixer_in, TOPK, axis=0)
    send_rows = (
        jnp.zeros((EXPERTS * CAP, width), jnp.bfloat16)
        .at[slot_index]
        .set(routed)
        .reshape(EXPERTS, CAP, width)
    )
    gate_up = w_gate_up[0]
    down_proj = w_down[0]
    received = lax.all_to_all(send_rows, "expert", split_axis=0, concat_axis=0, tiled=True)
    source_count = received.shape[0] // local_experts
    grouped = received.reshape(source_count, local_experts, received.shape[1], width)
    outputs = expert_rows(grouped, gate_up, down_proj)
    returned = send_back(outputs.reshape(received.shape))
    picked = (
        returned.reshape(EXPERTS * CAP, width)[slot_index]
        .astype(jnp.float32)
        .reshape(tok_rows, TOPK, width)
    )
    mixed = jnp.sum(picked * gate_weights[0][:, :, None], axis=1)
    result = (middle_wide + mixed).astype(jnp.bfloat16)
    handed = shifted_2(result, "section", 1)
    return handed[None]


LINE = 4
GROUP = 8


def greet(section_too):
    section, me = lax.axis_index("section"), lax.axis_index("expert")
    barrier = pltpu.get_barrier_semaphore()
    for step in range(1, GROUP):
        other = lax.rem(me + step, GROUP)
        pl.semaphore_signal(barrier, inc=1, device_id=(section, other), device_id_type=MESH)
    count = GROUP - 1
    if section_too:
        sections = lax.axis_size("section")
        for step in (1, sections - 1):
            other = lax.rem(section + step, sections)
            pl.semaphore_signal(barrier, inc=1, device_id=(other, me), device_id_type=MESH)
        count += 2
    pl.semaphore_wait(barrier, count)


def gather_line(z, rows, send_sems, recv_sems):
    section, me = lax.axis_index("section"), lax.axis_index("expert")
    x = lax.rem(me, 2)
    partner = z * 2 + 1 - x

    def copy(shard, to, way):
        return pltpu.make_async_remote_copy(
            src_ref=rows.at[shard],
            dst_ref=rows.at[shard],
            send_sem=send_sems.at[shard, way],
            recv_sem=recv_sems.at[shard],
            device_id=(section, to),
            device_id_type=MESH,
        )

    sent = []

    def send(shard, to, way):
        out = copy(shard, to, way)
        out.start()
        sent.append(out)

    own = z * 2 + x
    if z < LINE - 1:
        send(own, own + 2, 0)
    if z > 0:
        send(own, own - 2, 1)
    send(own, partner, 2)
    for far in range(1, LINE):
        if z - far >= 0:
            shard = (z - far) * 2 + x
            copy(shard, partner, 2).wait_recv()
            if z < LINE - 1:
                send(shard, own + 2, 0)
            send(shard, partner, 2)
        if z + far < LINE:
            shard = (z + far) * 2 + x
            copy(shard, partner, 2).wait_recv()
            if z > 0:
                send(shard, own - 2, 1)
            send(shard, partner, 2)

    def finish():
        for place in range(LINE):
            copy(place * 2 + 1 - x, partner, 2).wait_recv()
        for out in sent:
            out.wait_send()

    return finish


LINE_ORDER = ((3, 2, 1, 0), (3, 0, 2, 1), (0, 3, 1, 2), (0, 1, 2, 3))


def scatter_line(z, terms, from_pair, from_below, from_above, outgoing, pair_send, pair_recv,
                 line_send, below_recv, above_recv, total):
    section, me = lax.axis_index("section"), lax.axis_index("expert")
    x = lax.rem(me, 2)
    own = z * 2 + x
    partner = z * 2 + 1 - x
    pair_copies = {}
    for place in LINE_ORDER[z]:
        pair_copies[place] = pltpu.make_async_remote_copy(
            src_ref=terms.at[place * 2 + 1 - x],
            dst_ref=from_pair.at[place],
            send_sem=pair_send.at[place],
            recv_sem=pair_recv.at[place],
            device_id=(section, partner),
            device_id_type=MESH,
        )
        pair_copies[place].start()

    def line_copy(place, up):
        return pltpu.make_async_remote_copy(
            src_ref=outgoing.at[place],
            dst_ref=(from_below if up else from_above).at[place],
            send_sem=line_send.at[place],
            recv_sem=(below_recv if up else above_recv).at[place],
            device_id=(section, own + 2 if up else own - 2),
            device_id_type=MESH,
        )

    sent = []
    for place in LINE_ORDER[z]:
        pair_copies[place].wait_recv()
        parts = [terms.at[place * 2 + x], from_pair.at[place]]
        if place >= z and z > 0:
            line_copy(place, True).wait_recv()
            parts.append(from_below.at[place])
        if place <= z and z < LINE - 1:
            line_copy(place, False).wait_recv()
            parts.append(from_above.at[place])
        value = parts[0][...].astype(jnp.float32)
        for part in parts[1:]:
            value = value + part[...].astype(jnp.float32)
        if place == z:
            total[...] = value
        else:
            outgoing[place] = value.astype(jnp.bfloat16)
            out = line_copy(place, place > z)
            out.start()
            sent.append(out)
    for place in range(LINE):
        pair_copies[place].wait_send()
    for out in sent:
        out.wait_send()


def scatter_scratch(rows, width):
    slots = pltpu.VMEM((LINE, rows, width), jnp.bfloat16)
    sems = pltpu.SemaphoreType.DMA((LINE,))
    return [slots] * 4 + [sems] * 5 + [pltpu.VMEM((rows, width), jnp.float32)]


def remote(src, dst, send_sem, recv_sem, expert, section=None):
    if section is None:
        section = lax.axis_index("section")
    return pltpu.make_async_remote_copy(
        src_ref=src,
        dst_ref=dst,
        send_sem=send_sem,
        recv_sem=recv_sem,
        device_id=(section, expert),
        device_id_type=MESH,
    )


def at_place(body):
    me = lax.axis_index("expert")
    x = lax.rem(me, 2)
    for z in range(LINE):

        @pl.when(me // 2 == z)
        def _(z=z):
            body(z, x, z * 2 + x, z * 2 + 1 - x)


class Gather:
    def __init__(self, rows, send_sems, recv_sems):
        self.rows, self.send_sems, self.recv_sems = rows, send_sems, recv_sems

    def copy(self, chunk, shard, to, way):
        return remote(
            self.rows.at[chunk, shard], self.rows.at[chunk, shard],
            self.send_sems.at[chunk, shard, way], self.recv_sems.at[chunk, shard], to,
        )

    def first(self, chunk, z, own, partner):
        out = []
        if z < LINE - 1:
            out.append(self.copy(chunk, own, own + 2, 0))
        if z > 0:
            out.append(self.copy(chunk, own, own - 2, 1))
        return out + [self.copy(chunk, own, partner, 2)]

    def passing(self, chunk, z, x, own, partner):
        out = []
        for far in range(1, LINE):
            if z - far >= 0:
                shard = (z - far) * 2 + x
                onward = [self.copy(chunk, shard, own + 2, 0)] if z < LINE - 1 else []
                out.append((shard, onward + [self.copy(chunk, shard, partner, 2)]))
            if z + far < LINE:
                shard = (z + far) * 2 + x
                onward = [self.copy(chunk, shard, own - 2, 1)] if z > 0 else []
                out.append((shard, onward + [self.copy(chunk, shard, partner, 2)]))
        return out

    def start(self, chunk, z, x, own, partner):
        for out in self.first(chunk, z, own, partner):
            out.start()

    def forward(self, chunk, z, x, own, partner):
        for shard, onward in self.passing(chunk, z, x, own, partner):
            self.copy(chunk, shard, partner, 2).wait_recv()
            for out in onward:
                out.start()

    def arrive(self, chunk, z, x, own, partner):
        for place in range(LINE):
            self.copy(chunk, place * 2 + 1 - x, partner, 2).wait_recv()

    def drain(self, chunk, z, x, own, partner):
        for out in self.first(chunk, z, own, partner):
            out.wait_send()
        for _, onward in self.passing(chunk, z, x, own, partner):
            for out in onward:
                out.wait_send()


def opening_kernel(acts, gains, keyval, gates, rows, weights, all_gates,
                   send_sems, recv_sems, keyval_send, keyval_recv, pass_send, gate_send,
                   gate_recv, local_sem):
    section, me = lax.axis_index("section"), lax.axis_index("expert")
    rows[0, me] = rms_scale(acts[...].astype(jnp.float32), gains[0:1, :]).astype(jnp.bfloat16)
    greet(False)
    gather = Gather(rows, send_sems, recv_sems)
    own_gates = pltpu.make_async_copy(gates.at[me], all_gates.at[me], local_sem.at[1])
    own_weights = pltpu.make_async_copy(keyval.at[me // 2], weights.at[me], local_sem.at[0])
    gate_copies = []
    for step in range(1, GROUP):
        other = lax.rem(me + step, GROUP)
        gate_copies.append(
            remote(gates.at[other], all_gates.at[me], gate_send.at[step], gate_recv.at[step], other)
        )

    def line_weights(place, z, own):
        return remote(
            keyval.at[place], weights.at[own], keyval_send.at[place], keyval_recv.at[own],
            own + 2 * (place - z),
        )

    def pass_weights(place, z, x, partner):
        shard = place * 2 + x
        source = keyval.at[z] if place == z else weights.at[shard]
        return remote(source, weights.at[shard], pass_send.at[place], keyval_recv.at[shard], partner)

    def begin(z, x, own, partner):
        gather.start(0, z, x, own, partner)
        for place in LINE_ORDER[z]:
            if place != z:
                line_weights(place, z, own).start()
        pass_weights(z, z, x, partner).start()

    def through(z, x, own, partner):
        nearest = sorted((p for p in range(LINE) if p != z), key=lambda p: abs(p - z))
        for place, (shard, onward) in zip(nearest, gather.passing(0, z, x, own, partner)):
            gather.copy(0, shard, partner, 2).wait_recv()
            for out in onward:
                out.start()
            source = place * 2 + x
            remote(
                weights.at[source], weights.at[source], pass_send.at[place],
                keyval_recv.at[source], partner,
            ).wait_recv()
            pass_weights(place, z, x, partner).start()
        gather.arrive(0, z, x, own, partner)
        for place in range(LINE):
            source = place * 2 + 1 - x
            remote(
                weights.at[source], weights.at[source], pass_send.at[place],
                keyval_recv.at[source], partner,
            ).wait_recv()
        gather.drain(0, z, x, own, partner)
        for place in range(LINE):
            if place != z:
                line_weights(place, z, own).wait_send()
            pass_weights(place, z, x, partner).wait_send()

    at_place(begin)
    own_weights.start()
    own_gates.start()
    for out in gate_copies:
        out.start()
    at_place(through)
    for out in gate_copies:
        out.wait_recv()
    for out in gate_copies:
        out.wait_send()
    own_weights.wait()
    own_gates.wait()


def turning_kernel(terms, acts, gains, rows, middle,
                   from_pair, from_below, from_above, outgoing, pair_send, pair_recv,
                   line_send, below_recv, above_recv, total, send_sems, recv_sems):
    me = lax.axis_index("expert")
    greet(False)
    for z in range(LINE):

        @pl.when(me // 2 == z)
        def _(z=z):
            scatter_line(z, terms, from_pair, from_below, from_above, outgoing, pair_send,
                         pair_recv, line_send, below_recv, above_recv, total)
            joined = (acts[...].astype(jnp.float32) + total[...]).astype(jnp.bfloat16)
            middle[...] = joined
            rows[me] = rms_scale(joined.astype(jnp.float32), gains[1:2, :]).astype(jnp.bfloat16)
            gather_line(z, rows, send_sems, recv_sems)()


def closing_kernel(terms, middle, handed,
                   from_pair, from_below, from_above, outgoing, pair_send, pair_recv,
                   line_send, below_recv, above_recv, total, result, hand_send, hand_recv):
    section, me = lax.axis_index("section"), lax.axis_index("expert")
    greet(True)
    for z in range(LINE):

        @pl.when(me // 2 == z)
        def _(z=z):
            scatter_line(z, terms, from_pair, from_below, from_above, outgoing, pair_send,
                         pair_recv, line_send, below_recv, above_recv, total)

    result[...] = (middle[...].astype(jnp.float32) + total[...]).astype(jnp.bfloat16)
    hand = pltpu.make_async_remote_copy(
        src_ref=result,
        dst_ref=handed,
        send_sem=hand_send,
        recv_sem=hand_recv,
        device_id=(lax.rem(section + 1, lax.axis_size("section")), me),
        device_id_type=MESH,
    )
    hand.start()
    hand.wait()


def in_vmem(count):
    return [pl.BlockSpec(memory_space=pltpu.VMEM)] * count


def remote_params(collective_id, mebibytes):
    return pltpu.CompilerParams(
        collective_id=collective_id, has_side_effects=True, vmem_limit_bytes=mebibytes << 20
    )


def per_device(
    acts,
    norm_gains,
    w_query,
    w_keyval,
    w_out,
    w_gate_up,
    w_down,
    expert_ids,
    gate_weights,
    segment_ids,
):
    tok_rows, width = acts.shape[1:]
    head_dev = w_query.shape[2] // HD
    local_experts = w_gate_up.shape[1]
    gains = norm_gains[0]
    tokens = tok_rows * GROUP
    keyval = w_keyval[0].transpose(1, 0, 2)
    keyval_rows = keyval.shape[1]
    named = expert_ids[0][:, :, None] == jnp.arange(EXPERTS, dtype=jnp.int32)[None, None, :]
    dense_gates = jnp.sum(jnp.where(named, gate_weights[0][:, :, None], 0.0), axis=1)
    dense_gates = dense_gates.T.reshape(GROUP, local_experts, tok_rows)
    dma = pltpu.SemaphoreType.DMA
    row_piece, head_keyval, all_gates = pl.pallas_call(
        opening_kernel,
        out_shape=[
            jax.ShapeDtypeStruct((1, GROUP, tok_rows, width), jnp.bfloat16),
            jax.ShapeDtypeStruct((GROUP, keyval_rows, 2 * HD), jnp.bfloat16),
            jax.ShapeDtypeStruct(dense_gates.shape, jnp.float32),
        ],
        in_specs=in_vmem(4),
        out_specs=in_vmem(3),
        scratch_shapes=[
            dma((1, GROUP, 3)), dma((1, GROUP)), dma((LINE,)), dma((GROUP,)), dma((LINE,)),
            dma((GROUP,)), dma((GROUP,)), dma((2,)),
        ],
        compiler_params=remote_params(0, 8),
    )(acts[0], gains, keyval, dense_gates)
    row_piece = row_piece.reshape(tokens, width)
    head_keyval = head_keyval.reshape(width, 2 * HD)

    positions = jnp.arange(tokens).astype(jnp.float32)
    queries = jnp.dot(row_piece, w_query[0], preferred_element_type=jnp.float32)
    queries = rotate(queries.reshape(tokens, head_dev, HD), positions).astype(jnp.bfloat16)
    keyval_out = jnp.dot(row_piece, head_keyval, preferred_element_type=jnp.float32)
    key_rows = rotate(keyval_out[:, None, :HD], positions).astype(jnp.bfloat16).reshape(tokens, HD)
    value_rows = keyval_out[:, HD:].astype(jnp.bfloat16)
    segments = segment_ids[0]
    token_order = jnp.arange(tokens)
    attended = head_block(
        queries, key_rows, value_rows, segments, segments, token_order, token_order,
        1.0 / math.sqrt(HD),
    ).reshape(tokens, head_dev * HD)
    terms = jnp.dot(attended, w_out[0], preferred_element_type=jnp.float32).astype(jnp.bfloat16)
    mixer_rows, middle = pl.pallas_call(
        turning_kernel,
        out_shape=[
            jax.ShapeDtypeStruct((GROUP, tok_rows, width), jnp.bfloat16),
            jax.ShapeDtypeStruct((tok_rows, width), jnp.bfloat16),
        ],
        in_specs=in_vmem(3),
        out_specs=in_vmem(2),
        scratch_shapes=scatter_scratch(tok_rows, width) + [dma((GROUP, 3)), dma((GROUP,))],
        compiler_params=remote_params(1, 12),
    )(terms.reshape(GROUP, tok_rows, width), acts[0], gains)
    mixer_rows = mixer_rows.reshape(tokens, width)

    gates = all_gates.transpose(1, 0, 2).reshape(local_experts, tokens)
    member = gates > 0
    before = (token_order[:, None] < token_order[None, :]).astype(jnp.bfloat16)
    rank = jnp.dot(member.astype(jnp.bfloat16), before, preferred_element_type=jnp.float32)
    slots = GROUP * CAP
    slot_of = jnp.where(member, rank.astype(jnp.int32), -1)
    places = jnp.arange(slots, dtype=jnp.int32)
    chosen = slot_of[:, None, :] == places[None, :, None]
    slot_gates = jnp.sum(jnp.where(chosen, gates[:, None, :], 0.0), axis=2)
    chosen = chosen.astype(jnp.bfloat16)
    grouped = jnp.einsum(
        "est,td->esd", chosen, mixer_rows, preferred_element_type=jnp.float32
    ).astype(jnp.bfloat16)
    gate_up_out = jnp.einsum(
        "esd,edf->esf", grouped, w_gate_up[0], preferred_element_type=jnp.float32
    )
    ff = w_down.shape[2]
    hidden = (jax.nn.silu(gate_up_out[..., :ff]) * gate_up_out[..., ff:]).astype(jnp.bfloat16)
    outputs = jnp.einsum("esf,efd->esd", hidden, w_down[0], preferred_element_type=jnp.float32)
    outputs = (outputs * slot_gates[:, :, None]).astype(jnp.bfloat16)
    mixed = jnp.dot(
        chosen.reshape(local_experts * slots, tokens).T,
        outputs.reshape(local_experts * slots, width),
        preferred_element_type=jnp.float32,
    ).astype(jnp.bfloat16)

    handed = pl.pallas_call(
        closing_kernel,
        out_shape=jax.ShapeDtypeStruct((tok_rows, width), jnp.bfloat16),
        in_specs=in_vmem(2),
        out_specs=pl.BlockSpec(memory_space=pltpu.VMEM),
        scratch_shapes=scatter_scratch(tok_rows, width)
        + [pltpu.VMEM((tok_rows, width), jnp.bfloat16), dma, dma],
        compiler_params=remote_params(2, 10),
    )(mixed.reshape(GROUP, tok_rows, width), middle)
    return handed[None]


def solution(mesh):
    placed = (
        P("section", "expert", None),
        P("section", None, None),
        P("section", None, "expert"),
        P("section", "expert", None, None),
        P("section", "expert", None),
        P("section", "expert", None, None),
        P("section", "expert", None, None),
        P("section", "expert", None),
        P("section", "expert", None),
        P("section", None),
    )
    return jax.shard_map(
        per_device if mesh.shape["expert"] == GROUP else per_device_general,
        mesh=mesh,
        in_specs=placed,
        out_specs=P("section", "expert", None),
        check_vma=False,
    )
```

```python
import math

import jax
import jax.numpy as jnp
from jax import lax
from jax.experimental import pallas as pl
from jax.experimental.pallas import tpu as pltpu
from jax.sharding import PartitionSpec as P

MESH = pl.DeviceIdType.MESH

HD = 128
KV = 4
EXPERTS = 32
TOPK = 8
CAP = 24


EPS = 1e-06
ROPE_BASE = 1000000.0


def shifted_2(x, axis, by):
    length = lax.axis_size(axis)
    return lax.ppermute(x, axis, [(i, (i + by) % length) for i in range(length)])


def rms_scale(values, gain_row):
    mean_sq = jnp.mean(values * values, axis=-1, keepdims=True)
    return values * lax.rsqrt(mean_sq + EPS) * gain_row


def rotate(values, positions):
    half_width = values.shape[-1] // 2
    frequency = ROPE_BASE ** (-jnp.arange(half_width, dtype=jnp.float32) * 2.0 / values.shape[-1])
    angles = positions[:, None] * frequency[None, :]
    cosines = jnp.cos(angles)[:, None, :]
    sine_table = jnp.sin(angles)[:, None, :]
    leading = values[..., :half_width]
    trailing = values[..., half_width:]
    return jnp.concatenate(
        [leading * cosines - trailing * sine_table, trailing * cosines + leading * sine_table],
        axis=-1,
    )


def head_block(q_block, key_rows, value_rows, seg_block, seg_all, pos_block, pos_all, score_scale):
    scores = (
        jnp.einsum("qhd,kd->hqk", q_block, key_rows, preferred_element_type=jnp.float32)
        * score_scale
    )
    allowed = (seg_block[:, None] == seg_all[None, :]) & (pos_all[None, :] <= pos_block[:, None])
    scores = jnp.where(allowed[None], scores, -1e30)
    row_max = jnp.max(scores, axis=-1, keepdims=True)
    shifted = jnp.exp(scores - row_max)
    probability = (shifted / jnp.sum(shifted, axis=-1, keepdims=True)).astype(jnp.bfloat16)
    return jnp.einsum(
        "hqk,kd->qhd", probability, value_rows, preferred_element_type=jnp.float32
    ).astype(jnp.bfloat16)


def expert_rows(grouped, gate_up, down_proj):
    gate_up_out = jnp.einsum("necd,edf->necf", grouped, gate_up, preferred_element_type=jnp.float32)
    half_width = down_proj.shape[1]
    hidden = (jax.nn.silu(gate_up_out[..., :half_width]) * gate_up_out[..., half_width:]).astype(
        jnp.bfloat16
    )
    return jnp.einsum(
        "necf,efd->necd", hidden, down_proj, preferred_element_type=jnp.float32
    ).astype(jnp.bfloat16)


def send_back(results):
    return lax.all_to_all(results, "expert", split_axis=0, concat_axis=0, tiled=True)


def per_device_general(
    acts,
    norm_gains,
    w_query,
    w_keyval,
    w_out,
    w_gate_up,
    w_down,
    expert_ids,
    gate_weights,
    segment_ids,
):
    device_count = lax.axis_size("expert")
    my_index = lax.axis_index("expert")
    tok_rows = acts.shape[1]
    width = acts.shape[2]
    head_dev = w_query.shape[2] // HD
    local_experts = w_gate_up.shape[1]
    heads_total = head_dev * device_count
    gains = norm_gains[0]
    x_wide = acts[0].astype(jnp.float32)
    normed = rms_scale(x_wide, gains[0]).astype(jnp.bfloat16)
    kv_index = my_index * head_dev // (heads_total // KV)
    query_weight = w_query[0]
    gathered_keyval = lax.all_gather(w_keyval[0], "expert", axis=0, tiled=True)
    head_keyval = lax.dynamic_index_in_dim(gathered_keyval, kv_index, 1, keepdims=False)
    row_piece = lax.all_gather(normed, "expert", axis=0, tiled=True)
    piece_rows = row_piece.shape[0]
    positions = jnp.arange(piece_rows).astype(jnp.float32)
    query_piece_rows = row_piece.shape[0]
    query_positions = jnp.arange(query_piece_rows).astype(jnp.float32)
    queries = jnp.dot(row_piece, query_weight, preferred_element_type=jnp.float32).reshape(
        query_piece_rows, head_dev, HD
    )
    queries = (
        rotate(queries, query_positions)
        .astype(jnp.bfloat16)
        .reshape(query_piece_rows, head_dev * HD)
    )
    keyval = jnp.dot(row_piece, head_keyval, preferred_element_type=jnp.float32)
    key_rows = rotate(keyval[:, None, :HD], positions).astype(jnp.bfloat16).reshape(piece_rows, HD)
    value_rows = keyval[:, HD:].astype(jnp.bfloat16)
    projected = jnp.concatenate([queries, key_rows, value_rows], axis=1)
    tokens = projected.shape[0]
    all_queries = projected[:, : head_dev * HD].reshape(tokens, head_dev, HD)
    all_keys = projected[:, head_dev * HD : (head_dev + 1) * HD]
    all_values = projected[:, (head_dev + 1) * HD :]
    segments = segment_ids[0]
    all_positions = jnp.arange(tokens)
    q_rows = min(512, tokens)
    score_scale = 1.0 / math.sqrt(HD)

    def attend(first_row):
        q_block = lax.dynamic_slice_in_dim(all_queries, first_row, q_rows, 0)
        seg_block = lax.dynamic_slice_in_dim(segments, first_row, q_rows, 0)
        pos_block = first_row + jnp.arange(q_rows)
        return head_block(
            q_block,
            all_keys,
            all_values,
            seg_block,
            segments,
            pos_block,
            all_positions,
            score_scale,
        )

    block_starts = jnp.arange(tokens // q_rows) * q_rows
    attended = lax.map(attend, block_starts).reshape(tokens, head_dev * HD)
    out_weight = w_out[0]
    attention = lax.psum_scatter(
        jnp.dot(attended, out_weight, preferred_element_type=jnp.float32).astype(jnp.bfloat16),
        "expert",
        scatter_dimension=0,
        tiled=True,
    ).astype(jnp.float32)
    middle_wide = (x_wide + attention).astype(jnp.bfloat16).astype(jnp.float32)
    mixer_in = rms_scale(middle_wide, gains[1]).astype(jnp.bfloat16)
    routes_flat = expert_ids[0].reshape(-1)
    onehot = (routes_flat[:, None] == jnp.arange(EXPERTS, dtype=jnp.int32)[None, :]).astype(
        jnp.int32
    )
    earlier = jnp.cumsum(onehot, axis=0) - onehot
    slot_rank = jnp.sum(earlier * onehot, axis=1)
    slot_index = routes_flat * CAP + slot_rank
    routed = jnp.repeat(mixer_in, TOPK, axis=0)
    send_rows = (
        jnp.zeros((EXPERTS * CAP, width), jnp.bfloat16)
        .at[slot_index]
        .set(routed)
        .reshape(EXPERTS, CAP, width)
    )
    gate_up = w_gate_up[0]
    down_proj = w_down[0]
    received = lax.all_to_all(send_rows, "expert", split_axis=0, concat_axis=0, tiled=True)
    source_count = received.shape[0] // local_experts
    grouped = received.reshape(source_count, local_experts, received.shape[1], width)
    outputs = expert_rows(grouped, gate_up, down_proj)
    returned = send_back(outputs.reshape(received.shape))
    picked = (
        returned.reshape(EXPERTS * CAP, width)[slot_index]
        .astype(jnp.float32)
        .reshape(tok_rows, TOPK, width)
    )
    mixed = jnp.sum(picked * gate_weights[0][:, :, None], axis=1)
    result = (middle_wide + mixed).astype(jnp.bfloat16)
    handed = shifted_2(result, "section", 1)
    return handed[None]


LINE = 4
GROUP = 8
PARTS = 2


def greet(section_too):
    section, me = lax.axis_index("section"), lax.axis_index("expert")
    barrier = pltpu.get_barrier_semaphore()
    for step in range(1, GROUP):
        other = lax.rem(me + step, GROUP)
        pl.semaphore_signal(barrier, inc=1, device_id=(section, other), device_id_type=MESH)
    count = GROUP - 1
    if section_too:
        sections = lax.axis_size("section")
        for step in (1, sections - 1):
            other = lax.rem(section + step, sections)
            pl.semaphore_signal(barrier, inc=1, device_id=(other, me), device_id_type=MESH)
        count += 2
    pl.semaphore_wait(barrier, count)


LINE_ORDER = ((3, 2, 1, 0), (3, 0, 2, 1), (0, 3, 1, 2), (0, 1, 2, 3))


def scatter_line(z, terms, from_pair, from_below, from_above, outgoing, pair_send, pair_recv,
                 line_send, below_recv, above_recv, ready):
    section, me = lax.axis_index("section"), lax.axis_index("expert")
    x = lax.rem(me, 2)
    own = z * 2 + x
    partner = z * 2 + 1 - x
    order = [(place, part) for place in LINE_ORDER[z] for part in range(PARTS)]
    pair_copies = {
        (place, part): remote(
            terms.at[place * 2 + 1 - x, part], from_pair.at[place, part],
            pair_send.at[place, part], pair_recv.at[place, part], partner,
        )
        for place, part in order
    }
    for item in order:
        pair_copies[item].start()

    def line_copy(place, part, up):
        landing, sems = (from_below, below_recv) if up else (from_above, above_recv)
        return remote(
            outgoing.at[place, part], landing.at[place, part], line_send.at[place, part],
            sems.at[place, part], own + 2 if up else own - 2,
        )

    sent = []
    for place, part in order:
        pair_copies[place, part].wait_recv()
        pieces = [from_pair.at[place, part]]
        if place >= z and z > 0:
            line_copy(place, part, True).wait_recv()
            pieces.append(from_below.at[place, part])
        if place <= z and z < LINE - 1:
            line_copy(place, part, False).wait_recv()
            pieces.append(from_above.at[place, part])
        value = terms[place * 2 + x, part].astype(jnp.float32)
        for piece in pieces:
            value = value + piece[...].astype(jnp.float32)
        if place == z:
            ready(part, value)
        else:
            outgoing[place, part] = value.astype(jnp.bfloat16)
            out = line_copy(place, part, place > z)
            out.start()
            sent.append(out)
    return list(pair_copies.values()) + sent


def scatter_scratch(rows, width):
    slots = pltpu.VMEM((LINE, PARTS, rows // PARTS, width), jnp.bfloat16)
    sems = pltpu.SemaphoreType.DMA((LINE, PARTS))
    return [slots] * 4 + [sems] * 5


def remote(src, dst, send_sem, recv_sem, expert, section=None):
    if section is None:
        section = lax.axis_index("section")
    return pltpu.make_async_remote_copy(
        src_ref=src,
        dst_ref=dst,
        send_sem=send_sem,
        recv_sem=recv_sem,
        device_id=(section, expert),
        device_id_type=MESH,
    )


def at_place(body):
    me = lax.axis_index("expert")
    x = lax.rem(me, 2)
    for z in range(LINE):

        @pl.when(me // 2 == z)
        def _(z=z):
            body(z, x, z * 2 + x, z * 2 + 1 - x)


class Gather:
    def __init__(self, rows, send_sems, recv_sems):
        self.rows, self.send_sems, self.recv_sems = rows, send_sems, recv_sems

    def copy(self, chunk, shard, to, way):
        return remote(
            self.rows.at[shard, chunk], self.rows.at[shard, chunk],
            self.send_sems.at[chunk, shard, way], self.recv_sems.at[chunk, shard], to,
        )

    def first(self, chunk, z, own, partner):
        out = []
        if z < LINE - 1:
            out.append(self.copy(chunk, own, own + 2, 0))
        if z > 0:
            out.append(self.copy(chunk, own, own - 2, 1))
        return out + [self.copy(chunk, own, partner, 2)]

    def passing(self, chunk, z, x, own, partner):
        out = []
        for far in range(1, LINE):
            if z - far >= 0:
                shard = (z - far) * 2 + x
                onward = [self.copy(chunk, shard, own + 2, 0)] if z < LINE - 1 else []
                out.append((shard, onward + [self.copy(chunk, shard, partner, 2)]))
            if z + far < LINE:
                shard = (z + far) * 2 + x
                onward = [self.copy(chunk, shard, own - 2, 1)] if z > 0 else []
                out.append((shard, onward + [self.copy(chunk, shard, partner, 2)]))
        return out

    def start(self, chunk, z, x, own, partner):
        for out in self.first(chunk, z, own, partner):
            out.start()

    def forward(self, chunk, z, x, own, partner):
        for shard, onward in self.passing(chunk, z, x, own, partner):
            self.copy(chunk, shard, partner, 2).wait_recv()
            for out in onward:
                out.start()

    def arrive(self, chunk, z, x, own, partner):
        for place in range(LINE):
            self.copy(chunk, place * 2 + 1 - x, partner, 2).wait_recv()

    def drain(self, chunk, z, x, own, partner):
        for out in self.first(chunk, z, own, partner):
            out.wait_send()
        for _, onward in self.passing(chunk, z, x, own, partner):
            for out in onward:
                out.wait_send()


def opening_kernel(acts, gains, keyval, gates, rows, weights, all_gates,
                   send_sems, recv_sems, keyval_send, keyval_recv, pass_send, gate_send,
                   gate_recv, local_sem):
    section, me = lax.axis_index("section"), lax.axis_index("expert")
    for part in range(PARTS):
        rows[me, part] = rms_scale(acts[part].astype(jnp.float32), gains[0:1, :]).astype(
            jnp.bfloat16
        )
    greet(False)
    gather = Gather(rows, send_sems, recv_sems)
    own_gates = pltpu.make_async_copy(gates.at[me], all_gates.at[me], local_sem.at[1])
    own_weights = pltpu.make_async_copy(keyval.at[me // 2], weights.at[me], local_sem.at[0])
    gate_copies = []
    for step in range(1, GROUP):
        other = lax.rem(me + step, GROUP)
        gate_copies.append(
            remote(gates.at[other], all_gates.at[me], gate_send.at[step], gate_recv.at[step], other)
        )

    def line_weights(place, z, own):
        return remote(
            keyval.at[place], weights.at[own], keyval_send.at[place], keyval_recv.at[own],
            own + 2 * (place - z),
        )

    def pass_weights(place, z, x, partner):
        shard = place * 2 + x
        source = keyval.at[z] if place == z else weights.at[shard]
        return remote(source, weights.at[shard], pass_send.at[place], keyval_recv.at[shard], partner)

    def begin(z, x, own, partner):
        for part in range(PARTS):
            gather.start(part, z, x, own, partner)
        for place in LINE_ORDER[z]:
            if place != z:
                line_weights(place, z, own).start()
        pass_weights(z, z, x, partner).start()

    def through(z, x, own, partner):
        nearest = sorted((p for p in range(LINE) if p != z), key=lambda p: abs(p - z))
        hops = [gather.passing(part, z, x, own, partner) for part in range(PARTS)]
        for place, *arrivals in zip(nearest, *hops):
            for part, (shard, onward) in enumerate(arrivals):
                gather.copy(part, shard, partner, 2).wait_recv()
                for out in onward:
                    out.start()
            source = place * 2 + x
            remote(
                weights.at[source], weights.at[source], pass_send.at[place],
                keyval_recv.at[source], partner,
            ).wait_recv()
            pass_weights(place, z, x, partner).start()
        for part in range(PARTS):
            gather.arrive(part, z, x, own, partner)
        for place in range(LINE):
            source = place * 2 + 1 - x
            remote(
                weights.at[source], weights.at[source], pass_send.at[place],
                keyval_recv.at[source], partner,
            ).wait_recv()
        for part in range(PARTS):
            gather.drain(part, z, x, own, partner)
        for place in range(LINE):
            if place != z:
                line_weights(place, z, own).wait_send()
            pass_weights(place, z, x, partner).wait_send()

    at_place(begin)
    own_weights.start()
    own_gates.start()
    for out in gate_copies:
        out.start()
    at_place(through)
    for out in gate_copies:
        out.wait_recv()
    for out in gate_copies:
        out.wait_send()
    own_weights.wait()
    own_gates.wait()


def turning_kernel(terms, acts, gains, rows, middle,
                   from_pair, from_below, from_above, outgoing, pair_send, pair_recv,
                   line_send, below_recv, above_recv, send_sems, recv_sems):
    me = lax.axis_index("expert")
    greet(False)
    gather = Gather(rows, send_sems, recv_sems)

    def body(z, x, own, partner):
        def ready(part, total):
            joined = (acts[part].astype(jnp.float32) + total).astype(jnp.bfloat16)
            middle[part] = joined
            rows[me, part] = rms_scale(joined.astype(jnp.float32), gains[1:2, :]).astype(
                jnp.bfloat16
            )
            gather.start(part, z, x, own, partner)

        sent = scatter_line(z, terms, from_pair, from_below, from_above, outgoing, pair_send,
                            pair_recv, line_send, below_recv, above_recv, ready)
        for arrivals in zip(*(gather.passing(p, z, x, own, partner) for p in range(PARTS))):
            for part, (shard, onward) in enumerate(arrivals):
                gather.copy(part, shard, partner, 2).wait_recv()
                for out in onward:
                    out.start()
        for part in range(PARTS):
            gather.arrive(part, z, x, own, partner)
        for part in range(PARTS):
            gather.drain(part, z, x, own, partner)
        for out in sent:
            out.wait_send()

    at_place(body)


def closing_kernel(terms, middle, handed,
                   from_pair, from_below, from_above, outgoing, pair_send, pair_recv,
                   line_send, below_recv, above_recv, result, hand_send, hand_recv):
    section, me = lax.axis_index("section"), lax.axis_index("expert")
    greet(True)

    def hand(part):
        return remote(
            result.at[part], handed.at[part], hand_send.at[part], hand_recv.at[part],
            me, lax.rem(section + 1, lax.axis_size("section")),
        )

    def ready(part, total):
        result[part] = (middle[part].astype(jnp.float32) + total).astype(jnp.bfloat16)
        hand(part).start()

    def body(z, x, own, partner):
        sent = scatter_line(z, terms, from_pair, from_below, from_above, outgoing, pair_send,
                            pair_recv, line_send, below_recv, above_recv, ready)
        for out in sent:
            out.wait_send()

    at_place(body)
    for part in range(PARTS):
        hand(part).wait()


def in_vmem(count):
    return [pl.BlockSpec(memory_space=pltpu.VMEM)] * count


def remote_params(collective_id, mebibytes):
    return pltpu.CompilerParams(
        collective_id=collective_id, has_side_effects=True, vmem_limit_bytes=mebibytes << 20
    )


def per_device(
    acts,
    norm_gains,
    w_query,
    w_keyval,
    w_out,
    w_gate_up,
    w_down,
    expert_ids,
    gate_weights,
    segment_ids,
):
    tok_rows, width = acts.shape[1:]
    head_dev = w_query.shape[2] // HD
    local_experts = w_gate_up.shape[1]
    gains = norm_gains[0]
    own_acts = acts[0].reshape(PARTS, tok_rows // PARTS, width)
    tokens = tok_rows * GROUP
    keyval = w_keyval[0].transpose(1, 0, 2)
    keyval_rows = keyval.shape[1]
    named = expert_ids[0][:, :, None] == jnp.arange(EXPERTS, dtype=jnp.int32)[None, None, :]
    dense_gates = jnp.sum(jnp.where(named, gate_weights[0][:, :, None], 0.0), axis=1)
    dense_gates = dense_gates.T.reshape(GROUP, local_experts, tok_rows)
    dma = pltpu.SemaphoreType.DMA
    row_piece, head_keyval, all_gates = pl.pallas_call(
        opening_kernel,
        out_shape=[
            jax.ShapeDtypeStruct((GROUP, PARTS, tok_rows // PARTS, width), jnp.bfloat16),
            jax.ShapeDtypeStruct((GROUP, keyval_rows, 2 * HD), jnp.bfloat16),
            jax.ShapeDtypeStruct(dense_gates.shape, jnp.float32),
        ],
        in_specs=in_vmem(4),
        out_specs=in_vmem(3),
        scratch_shapes=[
            dma((PARTS, GROUP, 3)), dma((PARTS, GROUP)), dma((LINE,)), dma((GROUP,)), dma((LINE,)),
            dma((GROUP,)), dma((GROUP,)), dma((2,)),
        ],
        compiler_params=remote_params(0, 8),
    )(own_acts, gains, keyval, dense_gates)
    row_piece = row_piece.reshape(tokens, width)
    head_keyval = head_keyval.reshape(width, 2 * HD)

    positions = jnp.arange(tokens).astype(jnp.float32)
    queries = jnp.dot(row_piece, w_query[0], preferred_element_type=jnp.float32)
    queries = rotate(queries.reshape(tokens, head_dev, HD), positions).astype(jnp.bfloat16)
    keyval_out = jnp.dot(row_piece, head_keyval, preferred_element_type=jnp.float32)
    key_rows = rotate(keyval_out[:, None, :HD], positions).astype(jnp.bfloat16).reshape(tokens, HD)
    value_rows = keyval_out[:, HD:].astype(jnp.bfloat16)
    segments = segment_ids[0]
    token_order = jnp.arange(tokens)
    attended = head_block(
        queries, key_rows, value_rows, segments, segments, token_order, token_order,
        1.0 / math.sqrt(HD),
    ).reshape(tokens, head_dev * HD)
    terms = jnp.dot(attended, w_out[0], preferred_element_type=jnp.float32).astype(jnp.bfloat16)
    mixer_rows, middle = pl.pallas_call(
        turning_kernel,
        out_shape=[
            jax.ShapeDtypeStruct((GROUP, PARTS, tok_rows // PARTS, width), jnp.bfloat16),
            jax.ShapeDtypeStruct(own_acts.shape, jnp.bfloat16),
        ],
        in_specs=in_vmem(3),
        out_specs=in_vmem(2),
        scratch_shapes=scatter_scratch(tok_rows, width) + [dma((PARTS, GROUP, 3)), dma((PARTS, GROUP))],
        compiler_params=remote_params(1, 12),
    )(terms.reshape(GROUP, PARTS, tok_rows // PARTS, width), own_acts, gains)
    mixer_rows = mixer_rows.reshape(tokens, width)

    gates = all_gates.transpose(1, 0, 2).reshape(local_experts, tokens)
    member = gates > 0
    before = (token_order[:, None] < token_order[None, :]).astype(jnp.bfloat16)
    rank = jnp.dot(member.astype(jnp.bfloat16), before, preferred_element_type=jnp.float32)
    slots = GROUP * CAP
    slot_of = jnp.where(member, rank.astype(jnp.int32), -1)
    places = jnp.arange(slots, dtype=jnp.int32)
    chosen = slot_of[:, None, :] == places[None, :, None]
    slot_gates = jnp.sum(jnp.where(chosen, gates[:, None, :], 0.0), axis=2)
    chosen = chosen.astype(jnp.bfloat16)
    grouped = jnp.einsum(
        "est,td->esd", chosen, mixer_rows, preferred_element_type=jnp.float32
    ).astype(jnp.bfloat16)
    gate_up_out = jnp.einsum(
        "esd,edf->esf", grouped, w_gate_up[0], preferred_element_type=jnp.float32
    )
    ff = w_down.shape[2]
    hidden = (jax.nn.silu(gate_up_out[..., :ff]) * gate_up_out[..., ff:]).astype(jnp.bfloat16)
    outputs = jnp.einsum("esf,efd->esd", hidden, w_down[0], preferred_element_type=jnp.float32)
    outputs = (outputs * slot_gates[:, :, None]).astype(jnp.bfloat16)
    mixed = jnp.dot(
        chosen.reshape(local_experts * slots, tokens).T,
        outputs.reshape(local_experts * slots, width),
        preferred_element_type=jnp.float32,
    ).astype(jnp.bfloat16)

    handed = pl.pallas_call(
        closing_kernel,
        out_shape=jax.ShapeDtypeStruct(own_acts.shape, jnp.bfloat16),
        in_specs=in_vmem(2),
        out_specs=pl.BlockSpec(memory_space=pltpu.VMEM),
        scratch_shapes=scatter_scratch(tok_rows, width)
        + [pltpu.VMEM(own_acts.shape, jnp.bfloat16), dma((PARTS,)), dma((PARTS,))],
        compiler_params=remote_params(2, 10),
    )(mixed.reshape(GROUP, PARTS, tok_rows // PARTS, width), middle)
    return handed.reshape(1, tok_rows, width)


def solution(mesh):
    placed = (
        P("section", "expert", None),
        P("section", None, None),
        P("section", None, "expert"),
        P("section", "expert", None, None),
        P("section", "expert", None),
        P("section", "expert", None, None),
        P("section", "expert", None, None),
        P("section", "expert", None),
        P("section", "expert", None),
        P("section", None),
    )
    return jax.shard_map(
        per_device if mesh.shape["expert"] == GROUP else per_device_general,
        mesh=mesh,
        in_specs=placed,
        out_specs=P("section", "expert", None),
        check_vma=False,
    )
```
